128 devices in a mesh: ta: 4 (over x), ha: 4 (over y_hi, core), wa: 8 (over z, y_lo).
Axes of the slice: x: 4, y: 4 (y_hi: 2, y_lo: 2; y = y_hi * 2 + y_lo), z: 4, core: 2. Of those that a mesh axis runs over, the one named last changes fastest.
Arguments:
- tokens: bfloat16 [12, 32, 64, 1536], P('ta', 'ha', 'wa'), may hold values from -6 to 6
- modulation: float32 [3, 1536], replicated, may hold values from -4 to 4
- w_query: bfloat16 [1536, 1536], replicated
- w_key: bfloat16 [1536, 1536], replicated
- w_value: bfloat16 [1536, 1536], replicated, may hold values from -0.15625 to 0.15625
- w_out: bfloat16 [1536, 1536], replicated, may hold values from -0.15625 to 0.15625
- norm_q: float32 [1536], replicated, may hold values from 0.8 to 1.6
- norm_k: float32 [1536], replicated, may hold values from 0.8 to 1.6
Outputs:
- branch: bfloat16 [12, 32, 64, 1536], P('ta', 'ha', 'wa')
The draws below stay inside these ranges and needn't reach their ends.
All inputs are finite; a program needn't handle non-finite values.
Results may differ from the reference program's by a relative error of at most 0.0051.
Values may be sent and summed in bfloat16 or wider, within the bound.
A program may use at most 192 MiB of HBM per device.

```python
import jax
import jax.numpy as jnp
from jax import lax

HEADS = 12
HEAD_DIM = 128
D = 1536
TT = 3
TH = 8
TW = 8
NT = 12
NH = 32
NW = 64


def shared_draw(key, which):
    own = jax.random.normal(jax.random.fold_in(key, which), (D, D), jnp.float32)
    return own * D ** (-0.5)


def draw_w_query(key, part):
    return shared_draw(key, 1).astype(jnp.bfloat16)


def draw_w_key(key, part):
    return shared_draw(key, 2).astype(jnp.bfloat16)


def shard_levels(stream_key, shape, split, least, high):
    level, own = 1.0, jax.random.fold_in(stream_key, 6)
    for position, parts in split:
        steps = jnp.exp(jax.random.uniform(jax.random.fold_in(own, position), (parts,), jnp.float32, least / len(split), high / len(split)))
        level = level * jnp.repeat(steps, shape[position] // parts).reshape([-1 if axis == position else 1 for axis in range(len(shape))])
    return level


def noise(rng, shape, width, bound, pieces=(), kind=jnp.bfloat16):
    values = width * jax.random.normal(rng, shape, jnp.float32)
    if pieces:
        values = values * shard_levels(rng, shape, pieces, -0.22, 0.18)
    return jnp.clip(values, -bound, bound).astype(kind)


def setup_inputs(seed: int = 0) -> dict:
    keys = jax.random.split(jax.random.key(seed), 9)
    tokens = noise(keys[0], (NT, NH, NW, D), 1.0, 6.0, ((0, 4), (1, 4), (2, 8)))
    modulation = noise(keys[1], (3, D), 1.0, 4.0, (), jnp.float32)
    w_query = draw_w_query(jax.random.fold_in(keys[8], 71), 0)
    w_key = draw_w_key(jax.random.fold_in(keys[8], 71), 0)
    w_value = noise(keys[4], (D, D), D ** -0.5, 0.15625)
    w_out = noise(keys[5], (D, D), D ** -0.5, 0.15625)
    norm_q = jnp.clip(jax.random.uniform(keys[6], (D,), jnp.float32, 0.8, 1.6), 0.8, 1.6)
    norm_k = jnp.clip(jax.random.uniform(keys[7], (D,), jnp.float32, 0.8, 1.6), 0.8, 1.6)
    return dict(tokens=tokens, modulation=modulation, w_query=w_query, w_key=w_key, w_value=w_value, w_out=w_out, norm_q=norm_q, norm_k=norm_k)


def modulate(tokens, modulation):
    values = tokens.astype(jnp.float32)
    center = values - lax.optimization_barrier(jnp.mean(values, axis=-1, keepdims=True))
    spread = lax.optimization_barrier(jnp.mean(center * center, axis=-1, keepdims=True))
    return (center * lax.rsqrt(spread + 1e-06) * (1.0 + modulation[1]) + modulation[0]).astype(jnp.bfloat16)

def rms_gain(values, gain):
    return values * lax.rsqrt(lax.optimization_barrier(jnp.mean(values * values, axis=-1, keepdims=True)) + 1e-06) * gain

def rotate_pairs(values, frame_pos, row_pos, column_pos):
    half = HEAD_DIM // 2
    sixth = HEAD_DIM // 6
    first = half - 2 * sixth
    freq_first = 10000.0 ** (-jnp.arange(first, dtype=jnp.float32) / first)
    freq_rest = 10000.0 ** (-jnp.arange(sixth, dtype=jnp.float32) / sixth)
    shape = values.shape[:3]
    angle_frame = frame_pos[:, None] * freq_first
    angle_row = row_pos[:, None] * freq_rest
    angle_column = column_pos[:, None] * freq_rest
    angles = jnp.concatenate([jnp.broadcast_to(angle_frame[:, None, None, :], shape + (first,)), jnp.broadcast_to(angle_row[None, :, None, :], shape + (sixth,)), jnp.broadcast_to(angle_column[None, None, :, :], shape + (sixth,))], axis=-1)
    cosine = jnp.cos(angles)[:, :, :, None, :]
    sine = jnp.sin(angles)[:, :, :, None, :]
    pairs = values.reshape(shape + (HEADS, half, 2))
    even_part = pairs[..., 0]
    odd_part = pairs[..., 1]
    rotated = jnp.stack([even_part * cosine - odd_part * sine, even_part * sine + odd_part * cosine], axis=-1)
    return rotated.reshape(values.shape)

def tile_rows(query, key_pad, value_pad, anchor, extent):
    frame_count, row_count, column_count, width_all = query.shape
    tile_frames = frame_count // TT
    tile_rows_n = row_count // TH
    tile_columns = column_count // TW
    tile_size = TT * TH * TW
    window = 27 * tile_size

    def one_row(index):
        frame_tile = index // tile_rows_n
        row_tile = index % tile_rows_n
        zero = jnp.zeros((), jnp.int32)
        query_row = lax.dynamic_slice(query, (frame_tile * TT, row_tile * TH, zero, zero), (TT, TH, column_count, width_all))
        query_row = query_row.reshape(TT, TH, tile_columns, TW, HEADS, HEAD_DIM).transpose(4, 2, 0, 1, 3, 5)
        query_row = query_row.reshape(HEADS, tile_columns, tile_size, HEAD_DIM)
        key_win = lax.dynamic_slice(key_pad, (frame_tile * TT, row_tile * TH, zero, zero), (3 * TT, 3 * TH, column_count + 2 * TW, width_all))
        value_win = lax.dynamic_slice(value_pad, (frame_tile * TT, row_tile * TH, zero, zero), (3 * TT, 3 * TH, column_count + 2 * TW, width_all))
        key_tiles = jnp.stack([key_win[:, :, column * TW:column * TW + 3 * TW] for column in range(tile_columns)])
        value_tiles = jnp.stack([value_win[:, :, column * TW:column * TW + 3 * TW] for column in range(tile_columns)])
        key_tiles = key_tiles.reshape(tile_columns, window, HEADS, HEAD_DIM).transpose(2, 0, 1, 3)
        value_tiles = value_tiles.reshape(tile_columns, window, HEADS, HEAD_DIM).transpose(2, 0, 1, 3)
        frames_at = anchor[0] + frame_tile * TT - TT + jnp.arange(3 * TT, dtype=jnp.int32)
        rows_at = anchor[1] + row_tile * TH - TH + jnp.arange(3 * TH, dtype=jnp.int32)
        columns_at = anchor[2] + jnp.arange(tile_columns, dtype=jnp.int32)[:, None] * TW - TW + jnp.arange(3 * TW, dtype=jnp.int32)[None, :]
        frame_ok = (frames_at >= 0) & (frames_at < extent[0])
        row_ok = (rows_at >= 0) & (rows_at < extent[1])
        column_ok = (columns_at >= 0) & (columns_at < extent[2])
        valid = frame_ok[None, :, None, None] & row_ok[None, None, :, None] & column_ok[:, None, None, :]
        valid = valid.reshape(tile_columns, window)

        def one_head(operands):
            head_query, head_key, head_value = operands
            scores = jnp.einsum('cqd,ckd->cqk', head_query.astype(jnp.float32), head_key.astype(jnp.float32)) * HEAD_DIM ** (-0.5)
            scores = jnp.where(valid[:, None, :], scores, -1e+30)
            peak = lax.optimization_barrier(jnp.max(scores, axis=-1, keepdims=True))
            expo = jnp.exp(scores - peak)
            weights = (expo / lax.optimization_barrier(jnp.sum(expo, axis=-1, keepdims=True))).astype(jnp.bfloat16)
            return jnp.einsum('cqk,ckd->cqd', weights.astype(jnp.float32), head_value.astype(jnp.float32)).astype(jnp.bfloat16)
        attended = lax.map(one_head, (query_row, key_tiles, value_tiles))
        attended = attended.reshape(HEADS, tile_columns, TT, TH, TW, HEAD_DIM).transpose(2, 3, 1, 4, 0, 5)
        return attended.reshape(TT, TH, column_count, width_all)
    result = lax.map(one_row, jnp.arange(tile_frames * tile_rows_n, dtype=jnp.int32))
    result = result.reshape(tile_frames, tile_rows_n, TT, TH, column_count, width_all).transpose(0, 2, 1, 3, 4, 5)
    return result.reshape(frame_count, row_count, column_count, width_all)

def reference(tokens, modulation, w_query, w_key, w_value, w_out, norm_q, norm_k):
    normed = modulate(tokens, modulation)
    flat = normed.reshape(-1, D)
    grid = (NT, NH, NW, D)
    frame_pos = jnp.arange(NT, dtype=jnp.int32).astype(jnp.float32)
    row_pos = jnp.arange(NH, dtype=jnp.int32).astype(jnp.float32)
    column_pos = jnp.arange(NW, dtype=jnp.int32).astype(jnp.float32)
    query = rms_gain(jnp.dot(flat, w_query, preferred_element_type=jnp.float32), norm_q).reshape(grid)
    query = rotate_pairs(query, frame_pos, row_pos, column_pos).astype(jnp.bfloat16)
    key = rms_gain(jnp.dot(flat, w_key, preferred_element_type=jnp.float32), norm_k).reshape(grid)
    key = rotate_pairs(key, frame_pos, row_pos, column_pos).astype(jnp.bfloat16)
    value = jnp.dot(flat, w_value, preferred_element_type=jnp.float32).astype(jnp.bfloat16).reshape(grid)
    padding = ((TT, TT), (TH, TH), (TW, TW), (0, 0))
    key_pad = jnp.pad(key, padding)
    value_pad = jnp.pad(value, padding)
    attended = tile_rows(query, key_pad, value_pad, (0, 0, 0), (NT, NH, NW))
    branch = jnp.dot(attended.reshape(-1, D), w_out, preferred_element_type=jnp.float32) * modulation[2]
    return branch.astype(jnp.bfloat16).reshape(grid)
```

```python
import jax
import jax.numpy as jnp
import numpy as np
from jax import lax
from jax.experimental import pallas as pl
from jax.experimental.pallas import tpu as pltpu
from jax.sharding import PartitionSpec as P

HEADS = 12
HD = 128
D = 1536
N = 192
CHUNK = 256
NCHUNK = D // CHUNK
SLOTS = 9
OWN, WD, WZ, SIB, SIB_WD, SIB_WZ, AC_WD, AC, AC_WZ = range(SLOTS)
AHEAD = 2
MESH = pl.DeviceIdType.MESH
F32 = jnp.float32
BF16 = jnp.bfloat16


def angle_tables():
    half, sixth = HD // 2, HD // 6
    first = half - 2 * sixth
    freq_first = 10000.0 ** (-np.arange(first) / first)
    freq_rest = 10000.0 ** (-np.arange(sixth) / sixth)
    table = np.zeros((16, 8, 3, HD))
    for base, groups, size, start, freq in (
        (0, 4, 3, 0, freq_first),
        (4, 4, 8, first, freq_rest),
        (8, 8, 8, first + sixth, freq_rest),
    ):
        for group in range(groups):
            for row in range(size):
                angle = (group * size + row) * freq
                lanes = 2 * (start + np.arange(len(freq)))
                table[base + group, row, 0, lanes] = np.cos(angle)
                table[base + group, row, 0, lanes + 1] = np.cos(angle)
                table[base + group, row, 1, lanes] = -np.sin(angle)
                table[base + group, row, 2, lanes + 1] = np.sin(angle)
    return table.reshape(16, 8, 3 * HD).astype(np.float32)


def kernel(
    tok_ref, mod_ref, nq_ref, nk_ref, tab_ref, wq_hbm, wk_hbm, wv_hbm, wo_hbm,
    out_ref,
    wq, wk, wv, wo, xn, proj, cs, kv, ones, q, o_send, o_recv, o_own, st_send, st_recv, st_own, att,
    w_sem, kv_send, kv_recv, q_send, q_recv, o_ssem, o_rsem, st_ssem, st_rsem,
):
    ta, ha, wa = lax.axis_index("ta"), lax.axis_index("ha"), lax.axis_index("wa")
    edge = lax.rem(wa, 2)
    step = 2 - 4 * edge
    z_to, z_from = wa + step, wa - step
    has_to = jnp.logical_and(z_to >= 0, z_to < 8)
    has_from = jnp.logical_and(z_from >= 0, z_from < 8)
    inner = jnp.logical_and(ha >= 1, ha <= 2)
    inner_to = jnp.logical_and(inner, has_to)
    inner_from = jnp.logical_and(inner, has_from)
    has_prev, has_next = ta > 0, ta < 3
    direct = wa + 1 - 2 * edge
    sib = ha + 1 - 2 * lax.rem(ha, 2)
    dev_wd = (ta, ha, direct)
    dev_sib = (ta, sib, wa)
    dev_ac = (ta, 3 - ha, direct)
    dev_to = (ta, ha, z_to)
    dev_from = (ta, ha, z_from)
    dev_prev = (ta - 1, ha, wa)
    dev_next = (ta + 1, ha, wa)

    weights = ((wk_hbm, wk), (wv_hbm, wv), (wq_hbm, wq), (wo_hbm, wo))

    def weight_copy(which, c):
        hbm, buf = weights[which]
        return pltpu.make_async_copy(
            hbm.at[:, pl.ds(pl.multiple_of(c * CHUNK, CHUNK), CHUNK)], buf.at[c], w_sem.at[which, c]
        )

    for which in range(4):
        for c in range(NCHUNK):
            weight_copy(which, c).start()

    barrier = pltpu.get_barrier_semaphore()

    def greet(device):
        pl.semaphore_signal(barrier, inc=1, device_id=device, device_id_type=MESH)

    greet(dev_wd)
    greet(dev_sib)
    pl.when(has_to)(lambda: greet(dev_to))
    pl.when(has_from)(lambda: greet(dev_from))
    pl.when(inner)(lambda: greet(dev_ac))
    pl.when(has_prev)(lambda: greet(dev_prev))
    pl.when(has_next)(lambda: greet(dev_next))

    tf, tr, tc = tab_ref[ta], tab_ref[4 + ha], tab_ref[8 + wa]
    for f in range(3):
        for r in range(8):
            cs[pl.ds((f * 8 + r) * 8, 8), :] = tc + tr[r : r + 1, :] + tf[f : f + 1, :]

    scale = 1.0 + mod_ref[1:2, :]
    shift = mod_ref[0:1, :]
    for r in range(N // 32):
        rows = pl.ds(r * 32, 32)
        values = tok_ref[rows, :].astype(F32)
        center = values - jnp.mean(values, axis=-1, keepdims=True)
        spread = jnp.mean(center * center, axis=-1, keepdims=True)
        xn[rows, :] = (center * lax.rsqrt(spread + 1e-6) * scale + shift).astype(BF16)

    def project(which, store):
        def one(c, total):
            weight_copy(which, c).wait()
            acc = jnp.dot(xn[...], weights[which][1][c], preferred_element_type=F32)
            return store(c, acc, total)

        return lax.fori_loop(0, NCHUNK, one, jnp.zeros((N, HD), F32))

    def keep(c, acc, total):
        left, right = acc[:, :HD], acc[:, HD:]
        proj[2 * c] = left
        proj[2 * c + 1] = right
        return total + left * left + right * right

    def store_value(c, acc, total):
        kv[OWN, 2 * c, :, HD:] = acc[:, :HD].astype(BF16)
        kv[OWN, 2 * c + 1, :, HD:] = acc[:, HD:].astype(BF16)
        return total

    def rotated(h, inv, gain_ref):
        x = proj[h] * inv * gain_ref[h]
        return (
            x * cs[:, :HD]
            + pltpu.roll(x, HD - 1, 1) * cs[:, HD : 2 * HD]
            + pltpu.roll(x, 1, 1) * cs[:, 2 * HD :]
        ).astype(BF16)

    def inverse(total):
        return lax.rsqrt(jnp.sum(total, axis=-1, keepdims=True) * (1.0 / D) + 1e-6)

    own_wd = (0, OWN, WD, dev_wd)
    own_sib = (1, OWN, SIB, dev_sib)
    own_ac = (2, OWN, AC_WD, dev_ac)
    wd_to = (3, WD, WZ, dev_to)
    wd_sib = (4, WD, SIB_WD, dev_sib)
    wd_ac = (5, WD, AC, dev_ac)
    ac_to = (6, AC_WD, AC_WZ, dev_to)
    wz_sib = (7, WZ, SIB_WZ, dev_sib)

    def flow(which, h):
        index, source, target, device = which
        return pltpu.make_async_remote_copy(
            src_ref=kv.at[source, h],
            dst_ref=kv.at[target, h],
            send_sem=kv_send.at[index, h],
            recv_sem=kv_recv.at[index, h],
            device_id=device,
            device_id_type=MESH,
        )

    value_total = project(1, store_value)
    inv_k = inverse(project(0, keep))

    partners = (
        2
        + has_to.astype(jnp.int32)
        + has_from.astype(jnp.int32)
        + inner.astype(jnp.int32)
        + has_prev.astype(jnp.int32)
        + has_next.astype(jnp.int32)
    )
    pl.semaphore_wait(barrier, partners)

    @pl.loop(0, HEADS)
    def _(h):
        kv[OWN, h, :, :HD] = rotated(h, inv_k, nk_ref)
        flow(own_wd, h).start()
        pl.when(inner)(lambda: flow(own_ac, h).start())
        flow(own_sib, h).start()

    def absent(slot):
        ones[slot] = jnp.zeros((N, HD), BF16)

        @pl.loop(0, HEADS)
        def _(h):
            kv[slot, h, :, :HD] = kv[OWN, h, :, :HD]
            kv[slot, h, :, HD:] = jnp.zeros((N, HD), BF16)

    for slot in range(SLOTS):
        ones[slot] = jnp.ones((N, HD), BF16)

    @pl.when(jnp.logical_not(has_from))
    def _():
        absent(WZ)
        absent(SIB_WZ)

    @pl.when(jnp.logical_not(inner))
    def _():
        absent(AC_WD)
        absent(AC)

    @pl.when(jnp.logical_not(inner_from))
    def _():
        absent(AC_WZ)

    @pl.when(jnp.logical_not(has_prev))
    def _():
        q[1] = jnp.zeros((HEADS, N, HD), BF16)
        o_recv[0] = jnp.zeros((HEADS, N, HD), BF16)
        st_recv[0] = jnp.full((N, HD), -1e30, F32)

    @pl.when(jnp.logical_not(has_next))
    def _():
        q[2] = jnp.zeros((HEADS, N, HD), BF16)
        o_recv[1] = jnp.zeros((HEADS, N, HD), BF16)
        st_recv[1] = jnp.full((N, HD), -1e30, F32)

    def query_flow(which, h):
        return pltpu.make_async_remote_copy(
            src_ref=q.at[0, h],
            dst_ref=q.at[1 + which, h],
            send_sem=q_send.at[which, h],
            recv_sem=q_recv.at[which, h],
            device_id=(dev_next, dev_prev)[which],
            device_id_type=MESH,
        )

    def result_flow(which, h):
        return pltpu.make_async_remote_copy(
            src_ref=o_send.at[which, h],
            dst_ref=o_recv.at[1 - which, h],
            send_sem=o_ssem.at[which, h],
            recv_sem=o_rsem.at[1 - which, h],
            device_id=(dev_prev, dev_next)[which],
            device_id_type=MESH,
        )

    def stat_flow(which):
        return pltpu.make_async_remote_copy(
            src_ref=st_send.at[which],
            dst_ref=st_recv.at[1 - which],
            send_sem=st_ssem.at[which],
            recv_sem=st_rsem.at[1 - which],
            device_id=(dev_prev, dev_next)[which],
            device_id_type=MESH,
        )

    inv_q = inverse(project(2, keep))

    @pl.loop(0, HEADS)
    def _(h):
        q[0, h] = rotated(h, inv_q, nq_ref)
        pl.when(has_next)(lambda: query_flow(0, h).start())
        pl.when(has_prev)(lambda: query_flow(1, h).start())

    def pass_on(h):
        flow(own_wd, h).wait_recv()
        pl.when(has_to)(lambda: flow(wd_to, h).start())
        pl.when(inner)(lambda: flow(wd_ac, h).start())
        flow(wd_sib, h).start()
        pl.when(inner)(lambda: flow(own_ac, h).wait_recv())
        pl.when(inner_to)(lambda: flow(ac_to, h).start())

    for h in range(AHEAD):
        pass_on(h)

    factor = HD ** (-0.5)
    lanes = lax.broadcasted_iota(jnp.int32, (N, HD), 1)
    st_send[...] = jnp.zeros((2, N, HD), F32)
    st_own[...] = jnp.zeros((N, HD), F32)

    @pl.loop(0, HEADS)
    def _(h):
        pl.when(h + AHEAD < HEADS)(lambda: pass_on(h + AHEAD))

        @pl.when(has_from)
        def _():
            flow(wd_to, h).wait_recv()
            flow(wz_sib, h).start()

        flow(own_sib, h).wait_recv()
        flow(wd_sib, h).wait_recv()
        pl.when(inner)(lambda: flow(wd_ac, h).wait_recv())
        pl.when(inner_from)(lambda: flow(ac_to, h).wait_recv())
        pl.when(has_from)(lambda: flow(wz_sib, h).wait_recv())
        pl.when(has_prev)(lambda: query_flow(0, h).wait_recv())
        pl.when(has_next)(lambda: query_flow(1, h).wait_recv())

        keys = kv[:, h, :, :HD].reshape(SLOTS * N, HD)
        values = jnp.concatenate(
            [kv[:, h, :, HD:].reshape(SLOTS * N, HD), ones[...].reshape(SLOTS * N, HD)], axis=1
        )
        for part in (1, 2, 0):
            scores = lax.dot_general(
                q[part, h], keys, (((1,), (1,)), ((), ())), preferred_element_type=F32
            )
            peak = jnp.max(scores, axis=-1, keepdims=True)
            expo = jnp.exp((scores - peak) * factor).astype(BF16)
            acc = jnp.dot(expo, values, preferred_element_type=F32)
            result = acc[:, :HD] / acc[:, HD:]
            stat = peak * factor + jnp.log(acc[:, HD:])
            if part == 0:
                o_own[h] = result
                st_own[...] = jnp.where(lanes == h, stat, st_own[...])
            else:
                o_send[part - 1, h] = result.astype(BF16)
                st_send[part - 1] = jnp.where(lanes == h, stat, st_send[part - 1])

        pl.when(has_prev)(lambda: result_flow(0, h).start())
        pl.when(has_next)(lambda: result_flow(1, h).start())

    pl.when(has_prev)(lambda: stat_flow(0).start())
    pl.when(has_next)(lambda: stat_flow(1).start())

    @pl.when(has_next)
    def _():
        stat_flow(0).wait_recv()

        @pl.loop(0, HEADS)
        def _(h):
            result_flow(0, h).wait_recv()

    @pl.when(has_prev)
    def _():
        stat_flow(1).wait_recv()

        @pl.loop(0, HEADS)
        def _(h):
            result_flow(1, h).wait_recv()

    top = jnp.maximum(jnp.maximum(st_recv[0], st_recv[1]), st_own[...])
    e_prev, e_next, e_own = jnp.exp(st_recv[0] - top), jnp.exp(st_recv[1] - top), jnp.exp(st_own[...] - top)
    total = 1.0 / (e_prev + e_next + e_own)
    e_prev, e_next, e_own = e_prev * total, e_next * total, e_own * total
    for h in range(HEADS):
        column = slice(h, h + 1)
        att[:, h * HD : (h + 1) * HD] = (
            e_own[:, column] * o_own[h]
            + e_prev[:, column] * o_recv[0, h].astype(F32)
            + e_next[:, column] * o_recv[1, h].astype(F32)
        ).astype(BF16)

    for c in range(NCHUNK):
        weight_copy(3, c).wait()
        columns = slice(c * CHUNK, (c + 1) * CHUNK)
        out_ref[:, columns] = (
            jnp.dot(att[...], wo[c], preferred_element_type=F32) * mod_ref[2:3, columns]
        ).astype(BF16)

    @pl.loop(0, HEADS)
    def _(h):
        flow(own_wd, h).wait_send()
        flow(own_sib, h).wait_send()
        flow(wd_sib, h).wait_send()

        @pl.when(inner)
        def _():
            flow(own_ac, h).wait_send()
            flow(wd_ac, h).wait_send()

        pl.when(has_to)(lambda: flow(wd_to, h).wait_send())
        pl.when(inner_to)(lambda: flow(ac_to, h).wait_send())
        pl.when(has_from)(lambda: flow(wz_sib, h).wait_send())

        @pl.when(has_next)
        def _():
            query_flow(0, h).wait_send()
            result_flow(1, h).wait_send()

        @pl.when(has_prev)
        def _():
            query_flow(1, h).wait_send()
            result_flow(0, h).wait_send()

    pl.when(has_prev)(lambda: stat_flow(0).wait_send())
    pl.when(has_next)(lambda: stat_flow(1).wait_send())


def body(tokens, modulation, w_query, w_key, w_value, w_out, norm_q, norm_k):
    vmem = pl.BlockSpec(memory_space=pltpu.VMEM)
    hbm = pl.BlockSpec(memory_space=pl.ANY)
    weight = pltpu.VMEM((NCHUNK, D, CHUNK), BF16)
    dma = pltpu.SemaphoreType.DMA
    result = pl.pallas_call(
        kernel,
        out_shape=jax.ShapeDtypeStruct((N, D), BF16),
        in_specs=[vmem] * 5 + [hbm] * 4,
        out_specs=vmem,
        scratch_shapes=[
            weight, weight, weight, weight,
            pltpu.VMEM((N, D), BF16),
            pltpu.VMEM((HEADS, N, HD), F32),
            pltpu.VMEM((N, 3 * HD), F32),
            pltpu.VMEM((SLOTS, HEADS, N, 2 * HD), BF16),
            pltpu.VMEM((SLOTS, N, HD), BF16),
            pltpu.VMEM((3, HEADS, N, HD), BF16),
            pltpu.VMEM((2, HEADS, N, HD), BF16),
            pltpu.VMEM((2, HEADS, N, HD), BF16),
            pltpu.VMEM((HEADS, N, HD), F32),
            pltpu.VMEM((2, N, HD), F32),
            pltpu.VMEM((2, N, HD), F32),
            pltpu.VMEM((N, HD), F32),
            pltpu.VMEM((N, D), BF16),
            dma((4, NCHUNK)),
            dma((8, HEADS)), dma((8, HEADS)),
            dma((2, HEADS)), dma((2, HEADS)),
            dma((2, HEADS)), dma((2, HEADS)),
            dma((2,)), dma((2,)),
        ],
        compiler_params=pltpu.CompilerParams(
            collective_id=0, has_side_effects=True, vmem_limit_bytes=60 * 1024 * 1024
        ),
        name="tile_attention",
    )(
        tokens.reshape(N, D),
        modulation,
        norm_q.reshape(HEADS, 1, HD),
        norm_k.reshape(HEADS, 1, HD),
        jnp.asarray(angle_tables()),
        w_query, w_key, w_value, w_out,
    )
    return result.reshape(3, 8, 8, D)


def solution(mesh):
    in_specs = (P("ta", "ha", "wa", None), P(), P(), P(), P(), P(), P(), P())
    out_specs = P("ta", "ha", "wa", None)
    return jax.shard_map(body, mesh=mesh, in_specs=in_specs, out_specs=out_specs, check_vma=False)
```

```python
import jax
import jax.numpy as jnp
import numpy as np
from jax import lax
from jax.experimental import pallas as pl
from jax.experimental.pallas import tpu as pltpu
from jax.sharding import PartitionSpec as P

HEADS = 12
HD = 128
D = 1536
N = 192
CHUNK = 256
NCHUNK = D // CHUNK
SLOTS = 9
OWN, WD, WZ, SIB, SIB_WD, SIB_WZ, AC_WD, AC, AC_WZ = range(SLOTS)
AHEAD = 2
ROUND, TURN = 6, 3
MESH = pl.DeviceIdType.MESH
F32 = jnp.float32
BF16 = jnp.bfloat16


def angle_tables():
    half, sixth = HD // 2, HD // 6
    first = half - 2 * sixth
    freq_first = 10000.0 ** (-np.arange(first) / first)
    freq_rest = 10000.0 ** (-np.arange(sixth) / sixth)
    table = np.zeros((16, 8, 3, HD))
    for base, groups, size, start, freq in (
        (0, 4, 3, 0, freq_first),
        (4, 4, 8, first, freq_rest),
        (8, 8, 8, first + sixth, freq_rest),
    ):
        for group in range(groups):
            for row in range(size):
                angle = (group * size + row) * freq
                lanes = 2 * (start + np.arange(len(freq)))
                table[base + group, row, 0, lanes] = np.cos(angle)
                table[base + group, row, 0, lanes + 1] = np.cos(angle)
                table[base + group, row, 1, lanes] = -np.sin(angle)
                table[base + group, row, 2, lanes + 1] = np.sin(angle)
    return table.reshape(16, 8, 3 * HD).astype(np.float32)


def kernel(
    tok_ref, mod_ref, nq_ref, nk_ref, tab_ref, wq_hbm, wk_hbm, wv_hbm, wo_hbm,
    out_ref,
    wq, wk, wv, wo, xn, proj, cs, kv, transit, ones, q, o_send, o_recv, o_own, st_send, st_recv, st_parts, att,
    w_sem, kv_send, kv_recv, tr_send, tr_recv, q_send, q_recv, o_ssem, o_rsem, st_ssem, st_rsem,
):
    ta, ha, wa = lax.axis_index("ta"), lax.axis_index("ha"), lax.axis_index("wa")
    edge = lax.rem(wa, 2)
    step = 2 - 4 * edge
    z_to, z_from = wa + step, wa - step
    has_to = jnp.logical_and(z_to >= 0, z_to < 8)
    has_from = jnp.logical_and(z_from >= 0, z_from < 8)
    inner = jnp.logical_and(ha >= 1, ha <= 2)
    inner_to = jnp.logical_and(inner, has_to)
    inner_from = jnp.logical_and(inner, has_from)
    has_prev, has_next = ta > 0, ta < 3
    direct = wa + 1 - 2 * edge
    sib = ha + 1 - 2 * lax.rem(ha, 2)
    dev_wd = (ta, ha, direct)
    dev_sib = (ta, sib, wa)
    dev_ac = (ta, 3 - ha, direct)
    dev_to = (ta, ha, z_to)
    dev_from = (ta, ha, z_from)
    dev_prev = (ta - 1, ha, wa)
    dev_next = (ta + 1, ha, wa)

    weights = ((wk_hbm, wk), (wv_hbm, wv), (wq_hbm, wq), (wo_hbm, wo))

    def weight_copy(which, c):
        hbm, buf = weights[which]
        return pltpu.make_async_copy(
            hbm.at[:, pl.ds(pl.multiple_of(c * CHUNK, CHUNK), CHUNK)], buf.at[c], w_sem.at[which, c]
        )

    for which in range(4):
        for c in range(NCHUNK):
            weight_copy(which, c).start()

    barrier = pltpu.get_barrier_semaphore()

    def greet(device):
        pl.semaphore_signal(barrier, inc=1, device_id=device, device_id_type=MESH)

    greet(dev_wd)
    greet(dev_sib)
    pl.when(has_to)(lambda: greet(dev_to))
    pl.when(has_from)(lambda: greet(dev_from))
    pl.when(inner)(lambda: greet(dev_ac))
    pl.when(has_prev)(lambda: greet(dev_prev))
    pl.when(has_next)(lambda: greet(dev_next))

    tf, tr, tc = tab_ref[ta], tab_ref[4 + ha], tab_ref[8 + wa]
    for f in range(3):
        for r in range(8):
            cs[pl.ds((f * 8 + r) * 8, 8), :] = tc + tr[r : r + 1, :] + tf[f : f + 1, :]

    scale = 1.0 + mod_ref[1:2, :]
    shift = mod_ref[0:1, :]
    for r in range(N // 32):
        rows = pl.ds(r * 32, 32)
        values = tok_ref[rows, :].astype(F32)
        center = values - jnp.mean(values, axis=-1, keepdims=True)
        spread = jnp.mean(center * center, axis=-1, keepdims=True)
        xn[rows, :] = (center * lax.rsqrt(spread + 1e-6) * scale + shift).astype(BF16)

    def project(which, store):
        def one(c, total):
            weight_copy(which, c).wait()
            acc = jnp.dot(xn[...], weights[which][1][c], preferred_element_type=F32)
            return store(c, acc, total)

        return lax.fori_loop(0, NCHUNK, one, jnp.zeros((N, HD), F32))

    def keep(c, acc, total):
        left, right = acc[:, :HD], acc[:, HD:]
        proj[2 * c] = left
        proj[2 * c + 1] = right
        return total + left * left + right * right

    def rotated(h, inv, gain_ref):
        x = proj[h] * inv * gain_ref[pl.ds(pl.multiple_of(h * HD, HD), HD)].reshape(1, HD)
        return (
            x * cs[:, :HD]
            + pltpu.roll(x, HD - 1, 1) * cs[:, HD : 2 * HD]
            + pltpu.roll(x, 1, 1) * cs[:, 2 * HD :]
        ).astype(BF16)

    def inverse(total):
        return lax.rsqrt(jnp.sum(total, axis=-1, keepdims=True) * (1.0 / D) + 1e-6)

    own_wd = (0, OWN, WD, dev_wd)
    own_sib = (1, OWN, SIB, dev_sib)
    own_ac = (2, OWN, AC_WD, dev_ac)
    wd_to = (3, WD, WZ, dev_to)
    wd_sib = (4, WD, SIB_WD, dev_sib)
    wd_ac = (5, WD, AC, dev_ac)
    ac_to = (6, AC_WD, AC_WZ, dev_to)
    wz_sib = (7, WZ, SIB_WZ, dev_sib)

    def flow(which, h):
        index, source, target, device = which
        return pltpu.make_async_remote_copy(
            src_ref=kv.at[source, h],
            dst_ref=kv.at[target, h],
            send_sem=kv_send.at[index, h],
            recv_sem=kv_recv.at[index, h],
            device_id=device,
            device_id_type=MESH,
        )

    def turned(h):
        return h % ROUND == TURN

    def turn_flow(leg, h):
        k = h // ROUND
        source = kv.at[OWN, h] if leg == 0 else transit.at[k]
        target = (transit.at[k], kv.at[WZ, h], kv.at[AC_WZ, h])[leg]
        return pltpu.make_async_remote_copy(
            src_ref=source,
            dst_ref=target,
            send_sem=tr_send.at[leg, k],
            recv_sem=tr_recv.at[leg, k],
            device_id=(dev_from, dev_wd, dev_ac)[leg],
            device_id_type=MESH,
        )

    inv_k = inverse(project(0, keep))

    partners = (
        2
        + has_to.astype(jnp.int32)
        + has_from.astype(jnp.int32)
        + inner.astype(jnp.int32)
        + has_prev.astype(jnp.int32)
        + has_next.astype(jnp.int32)
    )
    pl.semaphore_wait(barrier, partners)

    def store_and_send(c, acc, total):
        for half in range(2):
            h = 2 * c + half
            kv[OWN, h, :, HD:] = acc[:, half * HD : (half + 1) * HD].astype(BF16)
            kv[OWN, h, :, :HD] = rotated(h, inv_k, nk_ref)
            flow(own_wd, h).start()
            pl.when(inner)(lambda: flow(own_ac, h).start())
            flow(own_sib, h).start()
            pl.when(jnp.logical_and(has_from, turned(h)))(lambda: turn_flow(0, h).start())
        return total

    project(1, store_and_send)

    def absent(slot):
        ones[slot] = jnp.zeros((N, HD), BF16)

        @pl.loop(0, HEADS)
        def _(h):
            kv[slot, h, :, :HD] = kv[OWN, h, :, :HD]
            kv[slot, h, :, HD:] = jnp.zeros((N, HD), BF16)

    for slot in range(SLOTS):
        ones[slot] = jnp.ones((N, HD), BF16)

    @pl.when(jnp.logical_not(has_from))
    def _():
        absent(WZ)
        absent(SIB_WZ)

    @pl.when(jnp.logical_not(inner))
    def _():
        absent(AC_WD)
        absent(AC)

    @pl.when(jnp.logical_not(inner_from))
    def _():
        absent(AC_WZ)

    @pl.when(jnp.logical_not(has_prev))
    def _():
        q[1] = jnp.zeros((HEADS, N, HD), BF16)
        o_recv[0] = jnp.zeros((HEADS, N, HD), BF16)
        st_recv[0] = jnp.full((16, 256), -1e30, F32)

    @pl.when(jnp.logical_not(has_next))
    def _():
        q[2] = jnp.zeros((HEADS, N, HD), BF16)
        o_recv[1] = jnp.zeros((HEADS, N, HD), BF16)
        st_recv[1] = jnp.full((16, 256), -1e30, F32)

    def query_flow(which, h):
        return pltpu.make_async_remote_copy(
            src_ref=q.at[0, h],
            dst_ref=q.at[1 + which, h],
            send_sem=q_send.at[which, h],
            recv_sem=q_recv.at[which, h],
            device_id=(dev_next, dev_prev)[which],
            device_id_type=MESH,
        )

    def result_flow(which, h):
        return pltpu.make_async_remote_copy(
            src_ref=o_send.at[which, h],
            dst_ref=o_recv.at[1 - which, h],
            send_sem=o_ssem.at[which, h],
            recv_sem=o_rsem.at[1 - which, h],
            device_id=(dev_prev, dev_next)[which],
            device_id_type=MESH,
        )

    def stat_flow(which):
        return pltpu.make_async_remote_copy(
            src_ref=st_send.at[which],
            dst_ref=st_recv.at[1 - which],
            send_sem=st_ssem.at[which],
            recv_sem=st_rsem.at[1 - which],
            device_id=(dev_prev, dev_next)[which],
            device_id_type=MESH,
        )

    inv_q = inverse(project(2, keep))

    @pl.loop(0, HEADS)
    def _(h):
        q[0, h] = rotated(h, inv_q, nq_ref)
        pl.when(has_next)(lambda: query_flow(0, h).start())
        pl.when(has_prev)(lambda: query_flow(1, h).start())

    def pass_on(h):
        flow(own_wd, h).wait_recv()
        turn = turned(h)
        straight = jnp.logical_not(turn)
        pl.when(jnp.logical_and(has_to, straight))(lambda: flow(wd_to, h).start())
        pl.when(inner)(lambda: flow(wd_ac, h).start())
        flow(wd_sib, h).start()
        pl.when(inner)(lambda: flow(own_ac, h).wait_recv())
        pl.when(jnp.logical_and(inner_to, straight))(lambda: flow(ac_to, h).start())

        @pl.when(jnp.logical_and(has_to, turn))
        def _():
            turn_flow(0, h).wait_recv()
            turn_flow(1, h).start()
            pl.when(inner)(lambda: turn_flow(2, h).start())

    for h in range(AHEAD):
        pass_on(h)

    factor = HD ** (-0.5)
    lanes = lax.broadcasted_iota(jnp.int32, (N, HD), 1)
    st_parts[...] = jnp.zeros((3, 256, HD), F32)

    @pl.loop(0, HEADS)
    def _(h):
        pl.when(h + AHEAD < HEADS)(lambda: pass_on(h + AHEAD))

        turn = turned(h)
        straight = jnp.logical_not(turn)

        @pl.when(has_from)
        def _():
            pl.when(straight)(lambda: flow(wd_to, h).wait_recv())
            pl.when(turn)(lambda: turn_flow(1, h).wait_recv())
            flow(wz_sib, h).start()

        flow(own_sib, h).wait_recv()
        flow(wd_sib, h).wait_recv()
        pl.when(inner)(lambda: flow(wd_ac, h).wait_recv())
        pl.when(jnp.logical_and(inner_from, straight))(lambda: flow(ac_to, h).wait_recv())
        pl.when(jnp.logical_and(inner_from, turn))(lambda: turn_flow(2, h).wait_recv())
        pl.when(has_from)(lambda: flow(wz_sib, h).wait_recv())
        pl.when(has_prev)(lambda: query_flow(0, h).wait_recv())
        pl.when(has_next)(lambda: query_flow(1, h).wait_recv())

        keys = kv[:, h, :, :HD].reshape(SLOTS * N, HD)
        values = jnp.concatenate(
            [kv[:, h, :, HD:].reshape(SLOTS * N, HD), ones[...].reshape(SLOTS * N, HD)], axis=1
        )
        def attend(part):
            scores = lax.dot_general(
                q[part, h], keys, (((1,), (1,)), ((), ())), preferred_element_type=F32
            )
            peak = jnp.max(scores, axis=-1, keepdims=True)
            expo = jnp.exp((scores - peak) * factor).astype(BF16)
            acc = jnp.dot(expo, values, preferred_element_type=F32)
            stat = peak * factor + jnp.log(acc[:, HD:])
            st_parts[part, :N] = jnp.where(lanes == h, stat, st_parts[part, :N])
            return acc[:, :HD] / acc[:, HD:]

        for part in (1, 2):
            o_send[part - 1, h] = attend(part).astype(BF16)
        pl.when(has_prev)(lambda: result_flow(0, h).start())
        pl.when(has_next)(lambda: result_flow(1, h).start())
        o_own[h] = attend(0)

    for which in range(2):
        st_send[which] = jnp.transpose(st_parts[1 + which])[:16]
    pl.when(has_prev)(lambda: stat_flow(0).start())
    pl.when(has_next)(lambda: stat_flow(1).start())

    @pl.when(has_next)
    def _():
        stat_flow(0).wait_recv()

        @pl.loop(0, HEADS)
        def _(h):
            result_flow(0, h).wait_recv()

    @pl.when(has_prev)
    def _():
        stat_flow(1).wait_recv()

        @pl.loop(0, HEADS)
        def _(h):
            result_flow(1, h).wait_recv()

    below = jnp.zeros((HD - 16, 256), F32)
    l_prev = jnp.transpose(jnp.concatenate([st_recv[0], below], axis=0))[:N]
    l_next = jnp.transpose(jnp.concatenate([st_recv[1], below], axis=0))[:N]
    l_own = st_parts[0, :N]
    top = jnp.maximum(jnp.maximum(l_prev, l_next), l_own)
    e_prev, e_next, e_own = jnp.exp(l_prev - top), jnp.exp(l_next - top), jnp.exp(l_own - top)
    total = 1.0 / (e_prev + e_next + e_own)
    e_prev, e_next, e_own = e_prev * total, e_next * total, e_own * total
    for h in range(HEADS):
        column = slice(h, h + 1)
        att[:, h * HD : (h + 1) * HD] = (
            e_own[:, column] * o_own[h]
            + e_prev[:, column] * o_recv[0, h].astype(F32)
            + e_next[:, column] * o_recv[1, h].astype(F32)
        ).astype(BF16)

    for c in range(NCHUNK):
        weight_copy(3, c).wait()
        columns = slice(c * CHUNK, (c + 1) * CHUNK)
        out_ref[:, columns] = (
            jnp.dot(att[...], wo[c], preferred_element_type=F32) * mod_ref[2:3, columns]
        ).astype(BF16)

    @pl.loop(0, HEADS)
    def _(h):
        flow(own_wd, h).wait_send()
        flow(own_sib, h).wait_send()
        flow(wd_sib, h).wait_send()

        @pl.when(inner)
        def _():
            flow(own_ac, h).wait_send()
            flow(wd_ac, h).wait_send()

        turn = turned(h)
        straight = jnp.logical_not(turn)
        pl.when(jnp.logical_and(has_to, straight))(lambda: flow(wd_to, h).wait_send())
        pl.when(jnp.logical_and(inner_to, straight))(lambda: flow(ac_to, h).wait_send())
        pl.when(jnp.logical_and(has_from, turn))(lambda: turn_flow(0, h).wait_send())
        pl.when(jnp.logical_and(has_to, turn))(lambda: turn_flow(1, h).wait_send())
        pl.when(jnp.logical_and(inner_to, turn))(lambda: turn_flow(2, h).wait_send())
        pl.when(has_from)(lambda: flow(wz_sib, h).wait_send())

        @pl.when(has_next)
        def _():
            query_flow(0, h).wait_send()
            result_flow(1, h).wait_send()

        @pl.when(has_prev)
        def _():
            query_flow(1, h).wait_send()
            result_flow(0, h).wait_send()

    pl.when(has_prev)(lambda: stat_flow(0).wait_send())
    pl.when(has_next)(lambda: stat_flow(1).wait_send())


def body(tokens, modulation, w_query, w_key, w_value, w_out, norm_q, norm_k):
    vmem = pl.BlockSpec(memory_space=pltpu.VMEM)
    hbm = pl.BlockSpec(memory_space=pl.ANY)
    weight = pltpu.VMEM((NCHUNK, D, CHUNK), BF16)
    dma = pltpu.SemaphoreType.DMA
    result = pl.pallas_call(
        kernel,
        out_shape=jax.ShapeDtypeStruct((N, D), BF16),
        in_specs=[vmem] * 5 + [hbm] * 4,
        out_specs=vmem,
        scratch_shapes=[
            weight, weight, weight, weight,
            pltpu.VMEM((N, D), BF16),
            pltpu.VMEM((HEADS, N, HD), F32),
            pltpu.VMEM((N, 3 * HD), F32),
            pltpu.VMEM((SLOTS, HEADS, N, 2 * HD), BF16),
            pltpu.VMEM((HEADS // ROUND, N, 2 * HD), BF16),
            pltpu.VMEM((SLOTS, N, HD), BF16),
            pltpu.VMEM((3, HEADS, N, HD), BF16),
            pltpu.VMEM((2, HEADS, N, HD), BF16),
            pltpu.VMEM((2, HEADS, N, HD), BF16),
            pltpu.VMEM((HEADS, N, HD), F32),
            pltpu.VMEM((2, 16, 256), F32),
            pltpu.VMEM((2, 16, 256), F32),
            pltpu.VMEM((3, 256, HD), F32),
            pltpu.VMEM((N, D), BF16),
            dma((4, NCHUNK)),
            dma((8, HEADS)), dma((8, HEADS)),
            dma((3, HEADS // ROUND)), dma((3, HEADS // ROUND)),
            dma((2, HEADS)), dma((2, HEADS)),
            dma((2, HEADS)), dma((2, HEADS)),
            dma((2,)), dma((2,)),
        ],
        compiler_params=pltpu.CompilerParams(
            collective_id=0, has_side_effects=True, vmem_limit_bytes=60 * 1024 * 1024
        ),
        name="tile_attention",
    )(
        tokens.reshape(N, D),
        modulation,
        norm_q,
        norm_k,
        jnp.asarray(angle_tables()),
        w_query, w_key, w_value, w_out,
    )
    return result.reshape(3, 8, 8, D)


def solution(mesh):
    in_specs = (P("ta", "ha", "wa", None), P(), P(), P(), P(), P(), P(), P())
    out_specs = P("ta", "ha", "wa", None)
    return jax.shard_map(body, mesh=mesh, in_specs=in_specs, out_specs=out_specs, check_vma=False)
```

```python
import jax
import jax.numpy as jnp
import numpy as np
from jax import lax
from jax.experimental import pallas as pl
from jax.experimental.pallas import tpu as pltpu
from jax.sharding import PartitionSpec as P

HEADS = 12
HD = 128
D = 1536
N = 192
CHUNK = 256
NCHUNK = D // CHUNK
SLOTS = 9
OWN, WD, WZ, SIB, SIB_WD, SIB_WZ, AC_WD, AC, AC_WZ = range(SLOTS)
AHEAD = 3
SHARE = 1
AT_ONCE = 4
TURN = 8
MESH = pl.DeviceIdType.MESH
F32 = jnp.float32
BF16 = jnp.bfloat16


def angle_tables():
    half, sixth = HD // 2, HD // 6
    first = half - 2 * sixth
    freq_first = 10000.0 ** (-np.arange(first) / first)
    freq_rest = 10000.0 ** (-np.arange(sixth) / sixth)
    table = np.zeros((16, 8, 3, HD))
    for base, groups, size, start, freq in (
        (0, 4, 3, 0, freq_first),
        (4, 4, 8, first, freq_rest),
        (8, 8, 8, first + sixth, freq_rest),
    ):
        for group in range(groups):
            for row in range(size):
                angle = (group * size + row) * freq
                lanes = 2 * (start + np.arange(len(freq)))
                table[base + group, row, 0, lanes] = np.cos(angle)
                table[base + group, row, 0, lanes + 1] = np.cos(angle)
                table[base + group, row, 1, lanes] = -np.sin(angle)
                table[base + group, row, 2, lanes + 1] = np.sin(angle)
    return table.reshape(16, 8, 3 * HD).astype(np.float32)


def kernel(
    tok_ref, mod_ref, nq_ref, nk_ref, tab_ref, wq_hbm, wk_hbm, wv_hbm, wo_hbm,
    out_ref,
    wq, wk, wv, wo, xn, proj, cs, kv, transit, ones, q, o_send, o_recv, o_own, st_send, st_recv, st_parts, att,
    w_sem, kv_send, kv_recv, tr_send, tr_recv, q_send, q_recv, o_ssem, o_rsem, st_ssem, st_rsem,
):
    ta, ha, wa = lax.axis_index("ta"), lax.axis_index("ha"), lax.axis_index("wa")
    edge = lax.rem(wa, 2)
    step = 2 - 4 * edge
    z_to, z_from = wa + step, wa - step
    has_to = jnp.logical_and(z_to >= 0, z_to < 8)
    has_from = jnp.logical_and(z_from >= 0, z_from < 8)
    inner = jnp.logical_and(ha >= 1, ha <= 2)
    inner_to = jnp.logical_and(inner, has_to)
    inner_from = jnp.logical_and(inner, has_from)
    has_prev, has_next = ta > 0, ta < 3
    direct = wa + 1 - 2 * edge
    sib = ha + 1 - 2 * lax.rem(ha, 2)
    dev_wd = (ta, ha, direct)
    dev_sib = (ta, sib, wa)
    dev_ac = (ta, 3 - ha, direct)
    dev_to = (ta, ha, z_to)
    dev_from = (ta, ha, z_from)
    dev_prev = (ta - 1, ha, wa)
    dev_next = (ta + 1, ha, wa)

    weights = ((wk_hbm, wk), (wv_hbm, wv), (wq_hbm, wq), (wo_hbm, wo))

    def weight_copy(which, c):
        hbm, buf = weights[which]
        return pltpu.make_async_copy(
            hbm.at[:, pl.ds(pl.multiple_of(c * CHUNK, CHUNK), CHUNK)], buf.at[c], w_sem.at[which, c]
        )

    for which in range(4):
        for c in range(NCHUNK):
            weight_copy(which, c).start()

    barrier = pltpu.get_barrier_semaphore()

    def greet(device):
        pl.semaphore_signal(barrier, inc=1, device_id=device, device_id_type=MESH)

    greet(dev_wd)
    greet(dev_sib)
    pl.when(has_to)(lambda: greet(dev_to))
    pl.when(has_from)(lambda: greet(dev_from))
    pl.when(inner)(lambda: greet(dev_ac))
    pl.when(has_prev)(lambda: greet(dev_prev))
    pl.when(has_next)(lambda: greet(dev_next))

    tf, tr, tc = tab_ref[ta], tab_ref[4 + ha], tab_ref[8 + wa]
    for f in range(3):
        for r in range(8):
            cs[pl.ds((f * 8 + r) * 8, 8), :] = tc + tr[r : r + 1, :] + tf[f : f + 1, :]

    scale = 1.0 + mod_ref[1:2, :]
    shift = mod_ref[0:1, :]
    for r in range(N // 32):
        rows = pl.ds(r * 32, 32)
        values = tok_ref[rows, :].astype(F32)
        center = values - jnp.mean(values, axis=-1, keepdims=True)
        spread = jnp.mean(center * center, axis=-1, keepdims=True)
        xn[rows, :] = (center * lax.rsqrt(spread + 1e-6) * scale + shift).astype(BF16)

    def project(which, store):
        def one(c, total):
            weight_copy(which, c).wait()
            acc = jnp.dot(xn[...], weights[which][1][c], preferred_element_type=F32)
            return store(c, acc, total)

        return lax.fori_loop(0, NCHUNK, one, jnp.zeros((N, HD), F32))

    def keep(c, acc, total):
        left, right = acc[:, :HD], acc[:, HD:]
        proj[2 * c] = left
        proj[2 * c + 1] = right
        return total + left * left + right * right

    def rotated(h, inv, gain_ref):
        x = proj[h] * inv * gain_ref[pl.ds(pl.multiple_of(h * HD, HD), HD)].reshape(1, HD)
        return (
            x * cs[:, :HD]
            + pltpu.roll(x, HD - 1, 1) * cs[:, HD : 2 * HD]
            + pltpu.roll(x, 1, 1) * cs[:, 2 * HD :]
        ).astype(BF16)

    def inverse(total):
        return lax.rsqrt(jnp.sum(total, axis=-1, keepdims=True) * (1.0 / D) + 1e-6)

    own_wd = (0, OWN, WD, dev_wd)
    own_sib = (1, OWN, SIB, dev_sib)
    own_ac = (2, OWN, AC_WD, dev_ac)
    wd_to = (3, WD, WZ, dev_to)
    wd_sib = (4, WD, SIB_WD, dev_sib)
    wd_ac = (5, WD, AC, dev_ac)
    ac_to = (6, AC_WD, AC_WZ, dev_to)
    wz_sib = (7, WZ, SIB_WZ, dev_sib)

    def flow(which, h):
        index, source, target, device = which
        return pltpu.make_async_remote_copy(
            src_ref=kv.at[source, h],
            dst_ref=kv.at[target, h],
            send_sem=kv_send.at[index, h],
            recv_sem=kv_recv.at[index, h],
            device_id=device,
            device_id_type=MESH,
        )

    def turned(h):
        return jnp.logical_and(h >= TURN, h % 2 == 0)

    def turn_flow(leg, h):
        k = (h - TURN) // 2
        source = kv.at[OWN, h] if leg == 0 else transit.at[k]
        target = (transit.at[k], kv.at[WZ, h], kv.at[AC_WZ, h])[leg]
        return pltpu.make_async_remote_copy(
            src_ref=source,
            dst_ref=target,
            send_sem=tr_send.at[leg, k],
            recv_sem=tr_recv.at[leg, k],
            device_id=(dev_from, dev_wd, dev_ac)[leg],
            device_id_type=MESH,
        )

    inv_k = inverse(project(0, keep))

    partners = (
        2
        + has_to.astype(jnp.int32)
        + has_from.astype(jnp.int32)
        + inner.astype(jnp.int32)
        + has_prev.astype(jnp.int32)
        + has_next.astype(jnp.int32)
    )
    pl.semaphore_wait(barrier, partners)

    def store_and_send(c, acc, total):
        for half in range(2):
            h = 2 * c + half
            kv[OWN, h, :, HD:] = acc[:, half * HD : (half + 1) * HD].astype(BF16)
            kv[OWN, h, :, :HD] = rotated(h, inv_k, nk_ref)
            flow(own_wd, h).start()
            pl.when(jnp.logical_and(inner, h < AT_ONCE))(lambda: flow(own_ac, h).start())
            flow(own_sib, h).start()
            pl.when(jnp.logical_and(has_from, turned(h)))(lambda: turn_flow(0, h).start())
        return total

    project(1, store_and_send)

    def absent(slot):
        ones[slot] = jnp.zeros((N, HD), BF16)

        @pl.loop(0, HEADS)
        def _(h):
            kv[slot, h, :, :HD] = kv[OWN, h, :, :HD]
            kv[slot, h, :, HD:] = jnp.zeros((N, HD), BF16)

    for slot in range(SLOTS):
        ones[slot] = jnp.ones((N, HD), BF16)

    @pl.when(jnp.logical_not(has_from))
    def _():
        absent(WZ)
        absent(SIB_WZ)

    @pl.when(jnp.logical_not(inner))
    def _():
        absent(AC_WD)
        absent(AC)

    @pl.when(jnp.logical_not(inner_from))
    def _():
        absent(AC_WZ)

    @pl.when(jnp.logical_not(has_prev))
    def _():
        q[1] = jnp.zeros((HEADS, N, HD), BF16)
        o_recv[0] = jnp.zeros((HEADS, N, HD), BF16)
        st_recv[0] = jnp.full((16, 256), -1e30, F32)

    @pl.when(jnp.logical_not(has_next))
    def _():
        q[2] = jnp.zeros((HEADS, N, HD), BF16)
        o_recv[1] = jnp.zeros((HEADS, N, HD), BF16)
        st_recv[1] = jnp.full((16, 256), -1e30, F32)

    def query_flow(which, h):
        return pltpu.make_async_remote_copy(
            src_ref=q.at[0, h],
            dst_ref=q.at[1 + which, h],
            send_sem=q_send.at[which, h],
            recv_sem=q_recv.at[which, h],
            device_id=(dev_next, dev_prev)[which],
            device_id_type=MESH,
        )

    def result_flow(which, h):
        return pltpu.make_async_remote_copy(
            src_ref=o_send.at[which, h],
            dst_ref=o_recv.at[1 - which, h],
            send_sem=o_ssem.at[which, h],
            recv_sem=o_rsem.at[1 - which, h],
            device_id=(dev_prev, dev_next)[which],
            device_id_type=MESH,
        )

    def stat_flow(which):
        return pltpu.make_async_remote_copy(
            src_ref=st_send.at[which],
            dst_ref=st_recv.at[1 - which],
            send_sem=st_ssem.at[which],
            recv_sem=st_rsem.at[1 - which],
            device_id=(dev_prev, dev_next)[which],
            device_id_type=MESH,
        )

    inv_q = inverse(project(2, keep))

    @pl.loop(0, HEADS)
    def _(h):
        q[0, h] = rotated(h, inv_q, nq_ref)
        pl.when(has_next)(lambda: query_flow(0, h).start())
        pl.when(has_prev)(lambda: query_flow(1, h).start())

    def pass_on(h):
        flow(own_wd, h).wait_recv()
        turn = turned(h)
        straight = jnp.logical_not(turn)
        pl.when(jnp.logical_and(has_to, straight))(lambda: flow(wd_to, h).start())
        pl.when(jnp.logical_and(inner, h + AT_ONCE < HEADS))(lambda: flow(own_ac, h + AT_ONCE).start())
        pl.when(inner)(lambda: flow(wd_ac, h).start())
        flow(wd_sib, h).start()
        pl.when(inner)(lambda: flow(own_ac, h).wait_recv())
        pl.when(jnp.logical_and(inner_to, straight))(lambda: flow(ac_to, h).start())

        @pl.when(jnp.logical_and(has_to, turn))
        def _():
            turn_flow(0, h).wait_recv()
            turn_flow(1, h).start()
            pl.when(inner)(lambda: turn_flow(2, h).start())

    def share(h):
        turn = turned(h)

        @pl.when(has_from)
        def _():
            pl.when(jnp.logical_not(turn))(lambda: flow(wd_to, h).wait_recv())
            pl.when(turn)(lambda: turn_flow(1, h).wait_recv())
            flow(wz_sib, h).start()

    for h in range(AHEAD):
        pass_on(h)
    for h in range(SHARE):
        share(h)

    factor = HD ** (-0.5)
    lanes = lax.broadcasted_iota(jnp.int32, (N, HD), 1)
    st_parts[...] = jnp.zeros((3, 256, HD), F32)

    @pl.loop(0, HEADS)
    def _(h):
        pl.when(h + AHEAD < HEADS)(lambda: pass_on(h + AHEAD))

        pl.when(h + SHARE < HEADS)(lambda: share(h + SHARE))
        turn = turned(h)
        straight = jnp.logical_not(turn)
        flow(own_sib, h).wait_recv()
        flow(wd_sib, h).wait_recv()
        pl.when(inner)(lambda: flow(wd_ac, h).wait_recv())
        pl.when(jnp.logical_and(inner_from, straight))(lambda: flow(ac_to, h).wait_recv())
        pl.when(jnp.logical_and(inner_from, turn))(lambda: turn_flow(2, h).wait_recv())
        pl.when(has_from)(lambda: flow(wz_sib, h).wait_recv())
        pl.when(has_prev)(lambda: query_flow(0, h).wait_recv())
        pl.when(has_next)(lambda: query_flow(1, h).wait_recv())

        keys = kv[:, h, :, :HD].reshape(SLOTS * N, HD)
        values = jnp.concatenate(
            [kv[:, h, :, HD:].reshape(SLOTS * N, HD), ones[...].reshape(SLOTS * N, HD)], axis=1
        )
        def attend(part):
            scores = lax.dot_general(
                q[part, h], keys, (((1,), (1,)), ((), ())), preferred_element_type=F32
            )
            peak = jnp.max(scores, axis=-1, keepdims=True)
            expo = jnp.exp((scores - peak) * factor).astype(BF16)
            acc = jnp.dot(expo, values, preferred_element_type=F32)
            stat = peak * factor + jnp.log(acc[:, HD:])
            st_parts[part, :N] = jnp.where(lanes == h, stat, st_parts[part, :N])
            return acc[:, :HD] / acc[:, HD:]

        for part in (1, 2):
            o_send[part - 1, h] = attend(part).astype(BF16)
        pl.when(has_prev)(lambda: result_flow(0, h).start())
        pl.when(has_next)(lambda: result_flow(1, h).start())
        o_own[h] = attend(0)

    for which in range(2):
        st_send[which] = jnp.transpose(st_parts[1 + which])[:16]
    pl.when(has_prev)(lambda: stat_flow(0).start())
    pl.when(has_next)(lambda: stat_flow(1).start())

    @pl.when(has_next)
    def _():
        stat_flow(0).wait_recv()

        @pl.loop(0, HEADS)
        def _(h):
            result_flow(0, h).wait_recv()

    @pl.when(has_prev)
    def _():
        stat_flow(1).wait_recv()

        @pl.loop(0, HEADS)
        def _(h):
            result_flow(1, h).wait_recv()

    below = jnp.zeros((HD - 16, 256), F32)
    l_prev = jnp.transpose(jnp.concatenate([st_recv[0], below], axis=0))[:N]
    l_next = jnp.transpose(jnp.concatenate([st_recv[1], below], axis=0))[:N]
    l_own = st_parts[0, :N]
    top = jnp.maximum(jnp.maximum(l_prev, l_next), l_own)
    e_prev, e_next, e_own = jnp.exp(l_prev - top), jnp.exp(l_next - top), jnp.exp(l_own - top)
    total = 1.0 / (e_prev + e_next + e_own)
    e_prev, e_next, e_own = e_prev * total, e_next * total, e_own * total
    for h in range(HEADS):
        column = slice(h, h + 1)
        att[:, h * HD : (h + 1) * HD] = (
            e_own[:, column] * o_own[h]
            + e_prev[:, column] * o_recv[0, h].astype(F32)
            + e_next[:, column] * o_recv[1, h].astype(F32)
        ).astype(BF16)

    for c in range(NCHUNK):
        weight_copy(3, c).wait()
        columns = slice(c * CHUNK, (c + 1) * CHUNK)
        out_ref[:, columns] = (
            jnp.dot(att[...], wo[c], preferred_element_type=F32) * mod_ref[2:3, columns]
        ).astype(BF16)

    @pl.loop(0, HEADS)
    def _(h):
        flow(own_wd, h).wait_send()
        flow(own_sib, h).wait_send()
        flow(wd_sib, h).wait_send()

        @pl.when(inner)
        def _():
            flow(own_ac, h).wait_send()
            flow(wd_ac, h).wait_send()

        turn = turned(h)
        straight = jnp.logical_not(turn)
        pl.when(jnp.logical_and(has_to, straight))(lambda: flow(wd_to, h).wait_send())
        pl.when(jnp.logical_and(inner_to, straight))(lambda: flow(ac_to, h).wait_send())
        pl.when(jnp.logical_and(has_from, turn))(lambda: turn_flow(0, h).wait_send())
        pl.when(jnp.logical_and(has_to, turn))(lambda: turn_flow(1, h).wait_send())
        pl.when(jnp.logical_and(inner_to, turn))(lambda: turn_flow(2, h).wait_send())
        pl.when(has_from)(lambda: flow(wz_sib, h).wait_send())

        @pl.when(has_next)
        def _():
            query_flow(0, h).wait_send()
            result_flow(1, h).wait_send()

        @pl.when(has_prev)
        def _():
            query_flow(1, h).wait_send()
            result_flow(0, h).wait_send()

    pl.when(has_prev)(lambda: stat_flow(0).wait_send())
    pl.when(has_next)(lambda: stat_flow(1).wait_send())


def body(tokens, modulation, w_query, w_key, w_value, w_out, norm_q, norm_k):
    vmem = pl.BlockSpec(memory_space=pltpu.VMEM)
    hbm = pl.BlockSpec(memory_space=pl.ANY)
    weight = pltpu.VMEM((NCHUNK, D, CHUNK), BF16)
    dma = pltpu.SemaphoreType.DMA
    result = pl.pallas_call(
        kernel,
        out_shape=jax.ShapeDtypeStruct((N, D), BF16),
        in_specs=[vmem] * 5 + [hbm] * 4,
        out_specs=vmem,
        scratch_shapes=[
            weight, weight, weight, weight,
            pltpu.VMEM((N, D), BF16),
            pltpu.VMEM((HEADS, N, HD), F32),
            pltpu.VMEM((N, 3 * HD), F32),
            pltpu.VMEM((SLOTS, HEADS, N, 2 * HD), BF16),
            pltpu.VMEM(((HEADS - TURN) // 2, N, 2 * HD), BF16),
            pltpu.VMEM((SLOTS, N, HD), BF16),
            pltpu.VMEM((3, HEADS, N, HD), BF16),
            pltpu.VMEM((2, HEADS, N, HD), BF16),
            pltpu.VMEM((2, HEADS, N, HD), BF16),
            pltpu.VMEM((HEADS, N, HD), F32),
            pltpu.VMEM((2, 16, 256), F32),
            pltpu.VMEM((2, 16, 256), F32),
            pltpu.VMEM((3, 256, HD), F32),
            pltpu.VMEM((N, D), BF16),
            dma((4, NCHUNK)),
            dma((8, HEADS)), dma((8, HEADS)),
            dma((3, (HEADS - TURN) // 2)), dma((3, (HEADS - TURN) // 2)),
            dma((2, HEADS)), dma((2, HEADS)),
            dma((2, HEADS)), dma((2, HEADS)),
            dma((2,)), dma((2,)),
        ],
        compiler_params=pltpu.CompilerParams(
            collective_id=0, has_side_effects=True, vmem_limit_bytes=60 * 1024 * 1024
        ),
        name="tile_attention",
    )(
        tokens.reshape(N, D),
        modulation,
        norm_q,
        norm_k,
        jnp.asarray(angle_tables()),
        w_query, w_key, w_value, w_out,
    )
    return result.reshape(3, 8, 8, D)


def solution(mesh):
    in_specs = (P("ta", "ha", "wa", None), P(), P(), P(), P(), P(), P(), P())
    out_specs = P("ta", "ha", "wa", None)
    return jax.shard_map(body, mesh=mesh, in_specs=in_specs, out_specs=out_specs, check_vma=False)
```

```python
import jax
import jax.numpy as jnp
import numpy as np
from jax import lax
from jax.experimental import pallas as pl
from jax.experimental.pallas import tpu as pltpu
from jax.sharding import PartitionSpec as P

HEADS = 12
HD = 128
D = 1536
N = 192
CHUNK = 256
NCHUNK = D // CHUNK
SLOTS = 9
OWN, WD, WZ, SIB, SIB_WD, SIB_WZ, AC_WD, AC, AC_WZ = range(SLOTS)
AHEAD = 3
SHARE = 1
AT_ONCE = 4
TURN = 8
AC_TURN = 4
EARLY = 10
MESH = pl.DeviceIdType.MESH
F32 = jnp.float32
BF16 = jnp.bfloat16


def angle_tables():
    half, sixth = HD // 2, HD // 6
    first = half - 2 * sixth
    freq_first = 10000.0 ** (-np.arange(first) / first)
    freq_rest = 10000.0 ** (-np.arange(sixth) / sixth)
    table = np.zeros((16, 8, 3, HD))
    for base, groups, size, start, freq in (
        (0, 4, 3, 0, freq_first),
        (4, 4, 8, first, freq_rest),
        (8, 8, 8, first + sixth, freq_rest),
    ):
        for group in range(groups):
            for row in range(size):
                angle = (group * size + row) * freq
                lanes = 2 * (start + np.arange(len(freq)))
                table[base + group, row, 0, lanes] = np.cos(angle)
                table[base + group, row, 0, lanes + 1] = np.cos(angle)
                table[base + group, row, 1, lanes] = -np.sin(angle)
                table[base + group, row, 2, lanes + 1] = np.sin(angle)
    return table.reshape(16, 8, 3 * HD).astype(np.float32)


def kernel(
    tok_ref, mod_ref, nq_ref, nk_ref, tab_ref, wq_hbm, wk_hbm, wv_hbm, wo_hbm,
    out_ref,
    wq, wk, wv, wo, xn, proj, cs, kv, transit, ones, q, o_send, o_recv, o_own, st_send, st_recv, st_parts, att,
    w_sem, kv_send, kv_recv, tr_send, tr_recv, q_send, q_recv, o_ssem, o_rsem, st_ssem, st_rsem,
):
    ta, ha, wa = lax.axis_index("ta"), lax.axis_index("ha"), lax.axis_index("wa")
    edge = lax.rem(wa, 2)
    step = 2 - 4 * edge
    z_to, z_from = wa + step, wa - step
    has_to = jnp.logical_and(z_to >= 0, z_to < 8)
    has_from = jnp.logical_and(z_from >= 0, z_from < 8)
    inner = jnp.logical_and(ha >= 1, ha <= 2)
    inner_to = jnp.logical_and(inner, has_to)
    inner_from = jnp.logical_and(inner, has_from)
    has_prev, has_next = ta > 0, ta < 3
    direct = wa + 1 - 2 * edge
    sib = ha + 1 - 2 * lax.rem(ha, 2)
    dev_wd = (ta, ha, direct)
    dev_sib = (ta, sib, wa)
    dev_ac = (ta, 3 - ha, direct)
    dev_to = (ta, ha, z_to)
    dev_from = (ta, ha, z_from)
    dev_prev = (ta - 1, ha, wa)
    dev_next = (ta + 1, ha, wa)

    weights = ((wk_hbm, wk), (wv_hbm, wv), (wq_hbm, wq), (wo_hbm, wo))

    def weight_copy(which, c):
        hbm, buf = weights[which]
        return pltpu.make_async_copy(
            hbm.at[:, pl.ds(pl.multiple_of(c * CHUNK, CHUNK), CHUNK)], buf.at[c], w_sem.at[which, c]
        )

    for which in range(4):
        for c in range(NCHUNK):
            weight_copy(which, c).start()

    barrier = pltpu.get_barrier_semaphore()

    def greet(device):
        pl.semaphore_signal(barrier, inc=1, device_id=device, device_id_type=MESH)

    greet(dev_wd)
    greet(dev_sib)
    pl.when(has_to)(lambda: greet(dev_to))
    pl.when(has_from)(lambda: greet(dev_from))
    pl.when(inner)(lambda: greet(dev_ac))
    pl.when(has_prev)(lambda: greet(dev_prev))
    pl.when(has_next)(lambda: greet(dev_next))

    tf, tr, tc = tab_ref[ta], tab_ref[4 + ha], tab_ref[8 + wa]
    for f in range(3):
        for r in range(8):
            cs[pl.ds((f * 8 + r) * 8, 8), :] = tc + tr[r : r + 1, :] + tf[f : f + 1, :]

    scale = 1.0 + mod_ref[1:2, :]
    shift = mod_ref[0:1, :]
    for r in range(N // 32):
        rows = pl.ds(r * 32, 32)
        values = tok_ref[rows, :].astype(F32)
        center = values - jnp.mean(values, axis=-1, keepdims=True)
        spread = jnp.mean(center * center, axis=-1, keepdims=True)
        xn[rows, :] = (center * lax.rsqrt(spread + 1e-6) * scale + shift).astype(BF16)

    def project(which, store):
        def one(c, total):
            weight_copy(which, c).wait()
            acc = jnp.dot(xn[...], weights[which][1][c], preferred_element_type=F32)
            return store(c, acc, total)

        return lax.fori_loop(0, NCHUNK, one, jnp.zeros((N, HD), F32))

    def keep(c, acc, total):
        left, right = acc[:, :HD], acc[:, HD:]
        proj[2 * c] = left
        proj[2 * c + 1] = right
        return total + left * left + right * right

    def rotated(h, inv, gain_ref):
        x = proj[h] * inv * gain_ref[pl.ds(pl.multiple_of(h * HD, HD), HD)].reshape(1, HD)
        return (
            x * cs[:, :HD]
            + pltpu.roll(x, HD - 1, 1) * cs[:, HD : 2 * HD]
            + pltpu.roll(x, 1, 1) * cs[:, 2 * HD :]
        ).astype(BF16)

    def inverse(total):
        return lax.rsqrt(jnp.sum(total, axis=-1, keepdims=True) * (1.0 / D) + 1e-6)

    own_wd = (0, OWN, WD, dev_wd)
    own_sib = (1, OWN, SIB, dev_sib)
    own_ac = (2, OWN, AC_WD, dev_ac)
    wd_to = (3, WD, WZ, dev_to)
    wd_sib = (4, WD, SIB_WD, dev_sib)
    wd_ac = (5, WD, AC, dev_ac)
    ac_to = (6, AC_WD, AC_WZ, dev_to)
    wz_sib = (7, WZ, SIB_WZ, dev_sib)

    def flow(which, h):
        index, source, target, device = which
        return pltpu.make_async_remote_copy(
            src_ref=kv.at[source, h],
            dst_ref=kv.at[target, h],
            send_sem=kv_send.at[index, h],
            recv_sem=kv_recv.at[index, h],
            device_id=device,
            device_id_type=MESH,
        )

    def turned(h):
        return jnp.logical_and(h >= TURN, h % 2 == 0)

    def ac_turned(h):
        return jnp.logical_and(h >= AC_TURN, h % 2 == 0)

    def in_transit(h):
        return jnp.logical_or(turned(h), jnp.logical_and(inner, ac_turned(h)))

    def turn_flow(leg, h):
        k = (h - AC_TURN) // 2
        source = kv.at[OWN, h] if leg == 0 else transit.at[k]
        target = (transit.at[k], kv.at[WZ, h], kv.at[AC_WZ, h])[leg]
        return pltpu.make_async_remote_copy(
            src_ref=source,
            dst_ref=target,
            send_sem=tr_send.at[leg, k],
            recv_sem=tr_recv.at[leg, k],
            device_id=(dev_from, dev_wd, dev_ac)[leg],
            device_id_type=MESH,
        )

    inv_k = inverse(project(0, keep))

    partners = (
        2
        + has_to.astype(jnp.int32)
        + has_from.astype(jnp.int32)
        + inner.astype(jnp.int32)
        + has_prev.astype(jnp.int32)
        + has_next.astype(jnp.int32)
    )
    pl.semaphore_wait(barrier, partners)

    def store_and_send(c, acc, total):
        for half in range(2):
            h = 2 * c + half
            kv[OWN, h, :, HD:] = acc[:, half * HD : (half + 1) * HD].astype(BF16)
            kv[OWN, h, :, :HD] = rotated(h, inv_k, nk_ref)
            flow(own_wd, h).start()
            pl.when(jnp.logical_and(inner, h < AT_ONCE))(lambda: flow(own_ac, h).start())
            flow(own_sib, h).start()
            pl.when(jnp.logical_and(has_from, in_transit(h)))(lambda: turn_flow(0, h).start())
        return total

    project(1, store_and_send)

    def absent(slot):
        ones[slot] = jnp.zeros((N, HD), BF16)

        @pl.loop(0, HEADS)
        def _(h):
            kv[slot, h, :, :HD] = kv[OWN, h, :, :HD]
            kv[slot, h, :, HD:] = jnp.zeros((N, HD), BF16)

    for slot in range(SLOTS):
        ones[slot] = jnp.ones((N, HD), BF16)

    @pl.when(jnp.logical_not(has_from))
    def _():
        absent(WZ)
        absent(SIB_WZ)

    @pl.when(jnp.logical_not(inner))
    def _():
        absent(AC_WD)
        absent(AC)

    @pl.when(jnp.logical_not(inner_from))
    def _():
        absent(AC_WZ)

    @pl.when(jnp.logical_not(has_prev))
    def _():
        q[1] = jnp.zeros((HEADS, N, HD), BF16)
        o_recv[0] = jnp.zeros((HEADS, N, HD), BF16)
        st_recv[:, 0] = jnp.full((2, 16, 256), -1e30, F32)

    @pl.when(jnp.logical_not(has_next))
    def _():
        q[2] = jnp.zeros((HEADS, N, HD), BF16)
        o_recv[1] = jnp.zeros((HEADS, N, HD), BF16)
        st_recv[:, 1] = jnp.full((2, 16, 256), -1e30, F32)

    def query_flow(which, h):
        return pltpu.make_async_remote_copy(
            src_ref=q.at[0, h],
            dst_ref=q.at[1 + which, h],
            send_sem=q_send.at[which, h],
            recv_sem=q_recv.at[which, h],
            device_id=(dev_next, dev_prev)[which],
            device_id_type=MESH,
        )

    def result_flow(which, h):
        return pltpu.make_async_remote_copy(
            src_ref=o_send.at[which, h],
            dst_ref=o_recv.at[1 - which, h],
            send_sem=o_ssem.at[which, h],
            recv_sem=o_rsem.at[1 - which, h],
            device_id=(dev_prev, dev_next)[which],
            device_id_type=MESH,
        )

    def stat_flow(stage, which):
        return pltpu.make_async_remote_copy(
            src_ref=st_send.at[stage, which],
            dst_ref=st_recv.at[stage, 1 - which],
            send_sem=st_ssem.at[stage, which],
            recv_sem=st_rsem.at[stage, 1 - which],
            device_id=(dev_prev, dev_next)[which],
            device_id_type=MESH,
        )

    inv_q = inverse(project(2, keep))

    @pl.loop(0, HEADS)
    def _(h):
        q[0, h] = rotated(h, inv_q, nq_ref)
        pl.when(has_next)(lambda: query_flow(0, h).start())
        pl.when(has_prev)(lambda: query_flow(1, h).start())

    def pass_on(h):
        flow(own_wd, h).wait_recv()
        turn, ac_turn = turned(h), ac_turned(h)
        pl.when(jnp.logical_and(has_to, jnp.logical_not(turn)))(lambda: flow(wd_to, h).start())
        pl.when(jnp.logical_and(inner, h + AT_ONCE < HEADS))(lambda: flow(own_ac, h + AT_ONCE).start())
        pl.when(inner)(lambda: flow(wd_ac, h).start())
        flow(wd_sib, h).start()
        pl.when(inner)(lambda: flow(own_ac, h).wait_recv())
        pl.when(jnp.logical_and(inner_to, jnp.logical_not(ac_turn)))(lambda: flow(ac_to, h).start())

        @pl.when(jnp.logical_and(has_to, in_transit(h)))
        def _():
            turn_flow(0, h).wait_recv()
            pl.when(turn)(lambda: turn_flow(1, h).start())
            pl.when(jnp.logical_and(inner, ac_turn))(lambda: turn_flow(2, h).start())

    def share(h):
        turn = turned(h)

        @pl.when(has_from)
        def _():
            pl.when(jnp.logical_not(turn))(lambda: flow(wd_to, h).wait_recv())
            pl.when(turn)(lambda: turn_flow(1, h).wait_recv())
            flow(wz_sib, h).start()

    for h in range(AHEAD):
        pass_on(h)
    for h in range(SHARE):
        share(h)

    factor = HD ** (-0.5) * float(np.log2(np.e))
    lanes = lax.broadcasted_iota(jnp.int32, (N, HD), 1)
    st_parts[...] = jnp.zeros((3, 256, HD), F32)

    def send_stats(stage):
        for which, has in ((0, has_prev), (1, has_next)):
            st_send[stage, which] = jnp.transpose(st_parts[1 + which])[:16]
            pl.when(has)(lambda: stat_flow(stage, which).start())

    @pl.loop(0, HEADS)
    def _(h):
        ahead = AHEAD + h + h // 2
        pl.when(ahead < HEADS)(lambda: pass_on(ahead))
        ac_turn = ac_turned(h)
        flow(own_sib, h).wait_recv()
        flow(wd_sib, h).wait_recv()
        pl.when(inner)(lambda: flow(wd_ac, h).wait_recv())
        pl.when(jnp.logical_and(inner_from, jnp.logical_not(ac_turn)))(lambda: flow(ac_to, h).wait_recv())
        pl.when(jnp.logical_and(inner_from, ac_turn))(lambda: turn_flow(2, h).wait_recv())
        pl.when(has_from)(lambda: flow(wz_sib, h).wait_recv())
        pl.when(has_prev)(lambda: query_flow(0, h).wait_recv())
        pl.when(has_next)(lambda: query_flow(1, h).wait_recv())

        keys = kv[:, h, :, :HD].reshape(SLOTS * N, HD)
        values = jnp.concatenate(
            [kv[:, h, :, HD:].reshape(SLOTS * N, HD), ones[...].reshape(SLOTS * N, HD)], axis=1
        )
        def attend(part):
            scores = lax.dot_general(
                q[part, h], keys, (((1,), (1,)), ((), ())), preferred_element_type=F32
            )
            peak = jnp.max(scores, axis=-1, keepdims=True)
            expo = jnp.exp2((scores - peak) * factor).astype(BF16)
            acc = jnp.dot(expo, values, preferred_element_type=F32)
            stat = peak * factor + jnp.log2(acc[:, HD:])
            st_parts[part, :N] = jnp.where(lanes == h, stat, st_parts[part, :N])
            return acc[:, :HD] / acc[:, HD:]

        for part in (1, 2):
            o_send[part - 1, h] = attend(part).astype(BF16)
        pl.when(has_prev)(lambda: result_flow(0, h).start())
        pl.when(has_next)(lambda: result_flow(1, h).start())
        pl.when(h + SHARE < HEADS)(lambda: share(h + SHARE))
        pl.when(jnp.logical_and(h % 2 == 1, ahead + 1 < HEADS))(lambda: pass_on(ahead + 1))
        o_own[h] = attend(0)

        pl.when(h == EARLY - 1)(lambda: send_stats(0))

    send_stats(1)

    def collect(stage, first, last):
        for which, has in ((0, has_next), (1, has_prev)):

            @pl.when(has)
            def _():
                stat_flow(stage, which).wait_recv()

                @pl.loop(first, last)
                def _(h):
                    result_flow(which, h).wait_recv()

        below = jnp.zeros((HD - 16, 256), F32)
        l_prev = jnp.transpose(jnp.concatenate([st_recv[stage, 0], below], axis=0))[:N]
        l_next = jnp.transpose(jnp.concatenate([st_recv[stage, 1], below], axis=0))[:N]
        l_own = st_parts[0, :N]
        top = jnp.maximum(jnp.maximum(l_prev, l_next), l_own)
        e_prev, e_next, e_own = jnp.exp2(l_prev - top), jnp.exp2(l_next - top), jnp.exp2(l_own - top)
        total = 1.0 / (e_prev + e_next + e_own)
        e_prev, e_next, e_own = e_prev * total, e_next * total, e_own * total
        for h in range(first, last):
            column = slice(h, h + 1)
            att[:, h * HD : (h + 1) * HD] = (
                e_own[:, column] * o_own[h]
                + e_prev[:, column] * o_recv[0, h].astype(F32)
                + e_next[:, column] * o_recv[1, h].astype(F32)
            ).astype(BF16)

    split = EARLY * HD
    collect(0, 0, EARLY)
    for c in range(NCHUNK):
        weight_copy(3, c).wait()
        acc = jnp.dot(att[:, :split], wo[c, :split], preferred_element_type=F32)
        proj[2 * c] = acc[:, :HD]
        proj[2 * c + 1] = acc[:, HD:]

    collect(1, EARLY, HEADS)
    for c in range(NCHUNK):
        columns = slice(c * CHUNK, (c + 1) * CHUNK)
        early = jnp.concatenate([proj[2 * c], proj[2 * c + 1]], axis=1)
        out_ref[:, columns] = (
            (early + jnp.dot(att[:, split:], wo[c, split:], preferred_element_type=F32)) * mod_ref[2:3, columns]
        ).astype(BF16)

    @pl.loop(0, HEADS)
    def _(h):
        flow(own_wd, h).wait_send()
        flow(own_sib, h).wait_send()
        flow(wd_sib, h).wait_send()

        @pl.when(inner)
        def _():
            flow(own_ac, h).wait_send()
            flow(wd_ac, h).wait_send()

        turn, ac_turn = turned(h), ac_turned(h)
        pl.when(jnp.logical_and(has_to, jnp.logical_not(turn)))(lambda: flow(wd_to, h).wait_send())
        pl.when(jnp.logical_and(inner_to, jnp.logical_not(ac_turn)))(lambda: flow(ac_to, h).wait_send())
        pl.when(jnp.logical_and(has_from, in_transit(h)))(lambda: turn_flow(0, h).wait_send())
        pl.when(jnp.logical_and(has_to, turn))(lambda: turn_flow(1, h).wait_send())
        pl.when(jnp.logical_and(inner_to, ac_turn))(lambda: turn_flow(2, h).wait_send())
        pl.when(has_from)(lambda: flow(wz_sib, h).wait_send())

        @pl.when(has_next)
        def _():
            query_flow(0, h).wait_send()
            result_flow(1, h).wait_send()

        @pl.when(has_prev)
        def _():
            query_flow(1, h).wait_send()
            result_flow(0, h).wait_send()

    for stage in range(2):
        pl.when(has_prev)(lambda: stat_flow(stage, 0).wait_send())
        pl.when(has_next)(lambda: stat_flow(stage, 1).wait_send())


def body(tokens, modulation, w_query, w_key, w_value, w_out, norm_q, norm_k):
    vmem = pl.BlockSpec(memory_space=pltpu.VMEM)
    hbm = pl.BlockSpec(memory_space=pl.ANY)
    weight = pltpu.VMEM((NCHUNK, D, CHUNK), BF16)
    dma = pltpu.SemaphoreType.DMA
    result = pl.pallas_call(
        kernel,
        out_shape=jax.ShapeDtypeStruct((N, D), BF16),
        in_specs=[vmem] * 5 + [hbm] * 4,
        out_specs=vmem,
        scratch_shapes=[
            weight, weight, weight, weight,
            pltpu.VMEM((N, D), BF16),
            pltpu.VMEM((HEADS, N, HD), F32),
            pltpu.VMEM((N, 3 * HD), F32),
            pltpu.VMEM((SLOTS, HEADS, N, 2 * HD), BF16),
            pltpu.VMEM(((HEADS - AC_TURN) // 2, N, 2 * HD), BF16),
            pltpu.VMEM((SLOTS, N, HD), BF16),
            pltpu.VMEM((3, HEADS, N, HD), BF16),
            pltpu.VMEM((2, HEADS, N, HD), BF16),
            pltpu.VMEM((2, HEADS, N, HD), BF16),
            pltpu.VMEM((HEADS, N, HD), F32),
            pltpu.VMEM((2, 2, 16, 256), F32),
            pltpu.VMEM((2, 2, 16, 256), F32),
            pltpu.VMEM((3, 256, HD), F32),
            pltpu.VMEM((N, D), BF16),
            dma((4, NCHUNK)),
            dma((8, HEADS)), dma((8, HEADS)),
            dma((3, (HEADS - AC_TURN) // 2)), dma((3, (HEADS - AC_TURN) // 2)),
            dma((2, HEADS)), dma((2, HEADS)),
            dma((2, HEADS)), dma((2, HEADS)),
            dma((2, 2)), dma((2, 2)),
        ],
        compiler_params=pltpu.CompilerParams(
            collective_id=0, has_side_effects=True, vmem_limit_bytes=60 * 1024 * 1024
        ),
        name="tile_attention",
    )(
        tokens.reshape(N, D),
        modulation,
        norm_q,
        norm_k,
        jnp.asarray(angle_tables()),
        w_query, w_key, w_value, w_out,
    )
    return result.reshape(3, 8, 8, D)


def solution(mesh):
    in_specs = (P("ta", "ha", "wa", None), P(), P(), P(), P(), P(), P(), P())
    out_specs = P("ta", "ha", "wa", None)
    return jax.shard_map(body, mesh=mesh, in_specs=in_specs, out_specs=out_specs, check_vma=False)
```

```python
import jax
import jax.numpy as jnp
import numpy as np
from jax import lax
from jax.experimental import pallas as pl
from jax.experimental.pallas import tpu as pltpu
from jax.sharding import PartitionSpec as P

HEADS = 12
HD = 128
D = 1536
N = 192
CHUNK = 256
NCHUNK = D // CHUNK
SLOTS = 9
OWN, WD, WZ, SIB, SIB_WD, SIB_WZ, AC_WD, AC, AC_WZ = range(SLOTS)
AHEAD = 3
SHARE = 1
AT_ONCE = 4
TURN = 8
AC_TURN = 4
EARLY = 10
MESH = pl.DeviceIdType.MESH
F32 = jnp.float32
BF16 = jnp.bfloat16


def angle_tables():
    half, sixth = HD // 2, HD // 6
    first = half - 2 * sixth
    freq_first = 10000.0 ** (-np.arange(first) / first)
    freq_rest = 10000.0 ** (-np.arange(sixth) / sixth)
    table = np.zeros((16, 8, 3, HD))
    for base, groups, size, start, freq in (
        (0, 4, 3, 0, freq_first),
        (4, 4, 8, first, freq_rest),
        (8, 8, 8, first + sixth, freq_rest),
    ):
        for group in range(groups):
            for row in range(size):
                angle = (group * size + row) * freq
                lanes = 2 * (start + np.arange(len(freq)))
                table[base + group, row, 0, lanes] = np.cos(angle)
                table[base + group, row, 0, lanes + 1] = np.cos(angle)
                table[base + group, row, 1, lanes] = -np.sin(angle)
                table[base + group, row, 2, lanes + 1] = np.sin(angle)
    return table.reshape(16, 8, 3 * HD).astype(np.float32)


def kernel(
    tok_ref, mod_ref, nq_ref, nk_ref, tab_ref, wq_hbm, wk_hbm, wv_hbm, wo_hbm,
    out_ref,
    wq, wk, wv, wo, xn, proj, cs, kv, transit, ones, q, o_send, o_recv, o_own, st_send, st_recv, st_parts, att,
    w_sem, kv_send, kv_recv, tr_send, tr_recv, q_send, q_recv, o_ssem, o_rsem, st_ssem, st_rsem,
):
    ta, ha, wa = lax.axis_index("ta"), lax.axis_index("ha"), lax.axis_index("wa")
    edge = lax.rem(wa, 2)
    step = 2 - 4 * edge
    z_to, z_from = wa + step, wa - step
    has_to = jnp.logical_and(z_to >= 0, z_to < 8)
    has_from = jnp.logical_and(z_from >= 0, z_from < 8)
    inner = jnp.logical_and(ha >= 1, ha <= 2)
    inner_to = jnp.logical_and(inner, has_to)
    inner_from = jnp.logical_and(inner, has_from)
    has_prev, has_next = ta > 0, ta < 3
    direct = wa + 1 - 2 * edge
    sib = ha + 1 - 2 * lax.rem(ha, 2)
    dev_wd = (ta, ha, direct)
    dev_sib = (ta, sib, wa)
    dev_ac = (ta, 3 - ha, direct)
    dev_to = (ta, ha, z_to)
    dev_from = (ta, ha, z_from)
    dev_prev = (ta - 1, ha, wa)
    dev_next = (ta + 1, ha, wa)

    weights = ((wk_hbm, wk), (wv_hbm, wv), (wq_hbm, wq), (wo_hbm, wo))

    def weight_copy(which, c):
        hbm, buf = weights[which]
        return pltpu.make_async_copy(
            hbm.at[:, pl.ds(pl.multiple_of(c * CHUNK, CHUNK), CHUNK)], buf.at[c], w_sem.at[which, c]
        )

    for which in range(4):
        for c in range(NCHUNK):
            weight_copy(which, c).start()

    barrier = pltpu.get_barrier_semaphore()

    def greet(device):
        pl.semaphore_signal(barrier, inc=1, device_id=device, device_id_type=MESH)

    greet(dev_wd)
    greet(dev_sib)
    pl.when(has_to)(lambda: greet(dev_to))
    pl.when(has_from)(lambda: greet(dev_from))
    pl.when(inner)(lambda: greet(dev_ac))
    pl.when(has_prev)(lambda: greet(dev_prev))
    pl.when(has_next)(lambda: greet(dev_next))

    tf, tr, tc = tab_ref[ta], tab_ref[4 + ha], tab_ref[8 + wa]
    for f in range(3):
        for r in range(8):
            cs[pl.ds((f * 8 + r) * 8, 8), :] = tc + tr[r : r + 1, :] + tf[f : f + 1, :]

    scale = 1.0 + mod_ref[1:2, :]
    shift = mod_ref[0:1, :]
    for r in range(N // 32):
        rows = pl.ds(r * 32, 32)
        values = tok_ref[rows, :].astype(F32)
        center = values - jnp.mean(values, axis=-1, keepdims=True)
        spread = jnp.mean(center * center, axis=-1, keepdims=True)
        xn[rows, :] = (center * lax.rsqrt(spread + 1e-6) * scale + shift).astype(BF16)

    def project(which, store):
        def one(c, total):
            weight_copy(which, c).wait()
            acc = jnp.dot(xn[...], weights[which][1][c], preferred_element_type=F32)
            return store(c, acc, total)

        return lax.fori_loop(0, NCHUNK, one, jnp.zeros((N, HD), F32))

    def keep(c, acc, total):
        left, right = acc[:, :HD], acc[:, HD:]
        proj[2 * c] = left
        proj[2 * c + 1] = right
        return total + left * left + right * right

    def rotated(h, inv, gain_ref):
        x = proj[h] * inv * gain_ref[pl.ds(pl.multiple_of(h * HD, HD), HD)].reshape(1, HD)
        return (
            x * cs[:, :HD]
            + pltpu.roll(x, HD - 1, 1) * cs[:, HD : 2 * HD]
            + pltpu.roll(x, 1, 1) * cs[:, 2 * HD :]
        ).astype(BF16)

    def inverse(total):
        return lax.rsqrt(jnp.sum(total, axis=-1, keepdims=True) * (1.0 / D) + 1e-6)

    own_wd = (0, OWN, WD, dev_wd)
    own_sib = (1, OWN, SIB, dev_sib)
    own_ac = (2, OWN, AC_WD, dev_ac)
    wd_to = (3, WD, WZ, dev_to)
    wd_sib = (4, WD, SIB_WD, dev_sib)
    wd_ac = (5, WD, AC, dev_ac)
    ac_to = (6, AC_WD, AC_WZ, dev_to)
    wz_sib = (7, WZ, SIB_WZ, dev_sib)

    def flow(which, h):
        index, source, target, device = which
        return pltpu.make_async_remote_copy(
            src_ref=kv.at[source, h],
            dst_ref=kv.at[target, h],
            send_sem=kv_send.at[index, h],
            recv_sem=kv_recv.at[index, h],
            device_id=device,
            device_id_type=MESH,
        )

    def turned(h):
        return jnp.logical_and(h >= TURN, h % 2 == 0)

    def ac_turned(h):
        return jnp.logical_and(h >= AC_TURN, h % 2 == 0)

    def in_transit(h):
        return jnp.logical_or(turned(h), jnp.logical_and(inner, ac_turned(h)))

    def turn_flow(leg, h):
        k = (h - AC_TURN) // 2
        source = kv.at[OWN, h] if leg == 0 else transit.at[k]
        target = (transit.at[k], kv.at[WZ, h], kv.at[AC_WZ, h])[leg]
        return pltpu.make_async_remote_copy(
            src_ref=source,
            dst_ref=target,
            send_sem=tr_send.at[leg, k],
            recv_sem=tr_recv.at[leg, k],
            device_id=(dev_from, dev_wd, dev_ac)[leg],
            device_id_type=MESH,
        )

    inv_k = inverse(project(0, keep))

    partners = (
        2
        + has_to.astype(jnp.int32)
        + has_from.astype(jnp.int32)
        + inner.astype(jnp.int32)
        + has_prev.astype(jnp.int32)
        + has_next.astype(jnp.int32)
    )
    pl.semaphore_wait(barrier, partners)

    def store_and_send(c, acc, total):
        for half in range(2):
            h = 2 * c + half
            kv[OWN, h, :, HD:] = acc[:, half * HD : (half + 1) * HD].astype(BF16)
            kv[OWN, h, :, :HD] = rotated(h, inv_k, nk_ref)
            flow(own_wd, h).start()
            pl.when(jnp.logical_and(inner, h < AT_ONCE))(lambda: flow(own_ac, h).start())
            flow(own_sib, h).start()
            pl.when(jnp.logical_and(has_from, in_transit(h)))(lambda: turn_flow(0, h).start())
        return total

    project(1, store_and_send)

    def absent(slot):
        ones[slot] = jnp.zeros((N, HD), BF16)

        @pl.loop(0, HEADS)
        def _(h):
            kv[slot, h, :, :HD] = kv[OWN, h, :, :HD]
            kv[slot, h, :, HD:] = jnp.zeros((N, HD), BF16)

    for slot in range(SLOTS):
        ones[slot] = jnp.ones((N, HD), BF16)

    @pl.when(jnp.logical_not(has_from))
    def _():
        absent(WZ)
        absent(SIB_WZ)

    @pl.when(jnp.logical_and(inner, jnp.logical_not(has_from)))
    def _():
        absent(AC_WZ)

    @pl.when(jnp.logical_not(has_prev))
    def _():
        q[1] = jnp.zeros((HEADS, N, HD), BF16)
        o_recv[0] = jnp.zeros((HEADS, N, HD), BF16)
        st_recv[:, 0] = jnp.full((2, 16, 256), -1e30, F32)

    @pl.when(jnp.logical_not(has_next))
    def _():
        q[2] = jnp.zeros((HEADS, N, HD), BF16)
        o_recv[1] = jnp.zeros((HEADS, N, HD), BF16)
        st_recv[:, 1] = jnp.full((2, 16, 256), -1e30, F32)

    def query_flow(which, h):
        return pltpu.make_async_remote_copy(
            src_ref=q.at[0, h],
            dst_ref=q.at[1 + which, h],
            send_sem=q_send.at[which, h],
            recv_sem=q_recv.at[which, h],
            device_id=(dev_next, dev_prev)[which],
            device_id_type=MESH,
        )

    def result_flow(which, h):
        return pltpu.make_async_remote_copy(
            src_ref=o_send.at[which, h],
            dst_ref=o_recv.at[1 - which, h],
            send_sem=o_ssem.at[which, h],
            recv_sem=o_rsem.at[1 - which, h],
            device_id=(dev_prev, dev_next)[which],
            device_id_type=MESH,
        )

    def stat_flow(stage, which):
        return pltpu.make_async_remote_copy(
            src_ref=st_send.at[stage, which],
            dst_ref=st_recv.at[stage, 1 - which],
            send_sem=st_ssem.at[stage, which],
            recv_sem=st_rsem.at[stage, 1 - which],
            device_id=(dev_prev, dev_next)[which],
            device_id_type=MESH,
        )

    def pass_on(h):
        flow(own_wd, h).wait_recv()
        turn, ac_turn = turned(h), ac_turned(h)
        pl.when(jnp.logical_and(has_to, jnp.logical_not(turn)))(lambda: flow(wd_to, h).start())
        pl.when(jnp.logical_and(inner, h + AT_ONCE < HEADS))(lambda: flow(own_ac, h + AT_ONCE).start())
        pl.when(inner)(lambda: flow(wd_ac, h).start())
        flow(wd_sib, h).start()
        pl.when(inner)(lambda: flow(own_ac, h).wait_recv())
        pl.when(jnp.logical_and(inner_to, jnp.logical_not(ac_turn)))(lambda: flow(ac_to, h).start())

        @pl.when(jnp.logical_and(has_to, in_transit(h)))
        def _():
            turn_flow(0, h).wait_recv()
            pl.when(turn)(lambda: turn_flow(1, h).start())
            pl.when(jnp.logical_and(inner, ac_turn))(lambda: turn_flow(2, h).start())

    def share(h):
        turn = turned(h)

        @pl.when(has_from)
        def _():
            pl.when(jnp.logical_not(turn))(lambda: flow(wd_to, h).wait_recv())
            pl.when(turn)(lambda: turn_flow(1, h).wait_recv())
            flow(wz_sib, h).start()

    inv_q = inverse(project(2, keep))
    pass_on(0)

    @pl.loop(0, HEADS // 2)
    def _(h):
        q[0, h] = rotated(h, inv_q, nq_ref)
        pl.when(has_next)(lambda: query_flow(0, h).start())
        pl.when(has_prev)(lambda: query_flow(1, h).start())

    pass_on(1)

    @pl.loop(HEADS // 2, HEADS)
    def _(h):
        q[0, h] = rotated(h, inv_q, nq_ref)
        pl.when(has_next)(lambda: query_flow(0, h).start())
        pl.when(has_prev)(lambda: query_flow(1, h).start())

    for h in range(2, AHEAD):
        pass_on(h)
    for h in range(SHARE):
        share(h)

    factor = HD ** (-0.5) * float(np.log2(np.e))
    lanes = lax.broadcasted_iota(jnp.int32, (N, HD), 1)
    st_parts[...] = jnp.zeros((3, 256, HD), F32)

    def send_stats(stage):
        for which, has in ((0, has_prev), (1, has_next)):
            st_send[stage, which] = jnp.transpose(st_parts[1 + which])[:16]
            pl.when(has)(lambda: stat_flow(stage, which).start())

    @pl.loop(0, HEADS)
    def _(h):
        ahead = AHEAD + h + h // 2
        pl.when(ahead < HEADS)(lambda: pass_on(ahead))
        ac_turn = ac_turned(h)
        flow(own_sib, h).wait_recv()
        flow(wd_sib, h).wait_recv()
        pl.when(inner)(lambda: flow(wd_ac, h).wait_recv())
        pl.when(jnp.logical_and(inner_from, jnp.logical_not(ac_turn)))(lambda: flow(ac_to, h).wait_recv())
        pl.when(jnp.logical_and(inner_from, ac_turn))(lambda: turn_flow(2, h).wait_recv())
        pl.when(has_from)(lambda: flow(wz_sib, h).wait_recv())
        pl.when(has_prev)(lambda: query_flow(0, h).wait_recv())
        pl.when(has_next)(lambda: query_flow(1, h).wait_recv())

        def attend(part, slots):
            keys = kv[:slots, h, :, :HD].reshape(slots * N, HD)
            values = jnp.concatenate(
                [kv[:slots, h, :, HD:].reshape(slots * N, HD), ones[:slots].reshape(slots * N, HD)], axis=1
            )
            scores = lax.dot_general(
                q[part, h], keys, (((1,), (1,)), ((), ())), preferred_element_type=F32
            )
            peak = jnp.max(scores, axis=-1, keepdims=True)
            expo = jnp.exp2((scores - peak) * factor).astype(BF16)
            acc = jnp.dot(expo, values, preferred_element_type=F32)
            stat = peak * factor + jnp.log2(acc[:, HD:])
            st_parts[part, :N] = jnp.where(lanes == h, stat, st_parts[part, :N])
            return acc[:, :HD] / acc[:, HD:]

        def other_frames(slots):
            for part in (1, 2):
                o_send[part - 1, h] = attend(part, slots).astype(BF16)

        def own_frames(slots):
            o_own[h] = attend(0, slots)

        pl.when(inner)(lambda: other_frames(SLOTS))
        pl.when(jnp.logical_not(inner))(lambda: other_frames(AC_WD))
        pl.when(has_prev)(lambda: result_flow(0, h).start())
        pl.when(has_next)(lambda: result_flow(1, h).start())
        pl.when(h + SHARE < HEADS)(lambda: share(h + SHARE))
        pl.when(jnp.logical_and(h % 2 == 1, ahead + 1 < HEADS))(lambda: pass_on(ahead + 1))
        pl.when(inner)(lambda: own_frames(SLOTS))
        pl.when(jnp.logical_not(inner))(lambda: own_frames(AC_WD))

        pl.when(h == EARLY - 1)(lambda: send_stats(0))

    send_stats(1)

    def collect(stage, first, last):
        for which, has in ((0, has_next), (1, has_prev)):

            @pl.when(has)
            def _():
                stat_flow(stage, which).wait_recv()

                @pl.loop(first, last)
                def _(h):
                    result_flow(which, h).wait_recv()

        below = jnp.zeros((HD - 16, 256), F32)
        l_prev = jnp.transpose(jnp.concatenate([st_recv[stage, 0], below], axis=0))[:N]
        l_next = jnp.transpose(jnp.concatenate([st_recv[stage, 1], below], axis=0))[:N]
        l_own = st_parts[0, :N]
        top = jnp.maximum(jnp.maximum(l_prev, l_next), l_own)
        e_prev, e_next, e_own = jnp.exp2(l_prev - top), jnp.exp2(l_next - top), jnp.exp2(l_own - top)
        total = 1.0 / (e_prev + e_next + e_own)
        e_prev, e_next, e_own = e_prev * total, e_next * total, e_own * total
        for h in range(first, last):
            column = slice(h, h + 1)
            att[:, h * HD : (h + 1) * HD] = (
                e_own[:, column] * o_own[h]
                + e_prev[:, column] * o_recv[0, h].astype(F32)
                + e_next[:, column] * o_recv[1, h].astype(F32)
            ).astype(BF16)

    split = EARLY * HD
    collect(0, 0, EARLY)
    for c in range(NCHUNK):
        weight_copy(3, c).wait()
        acc = jnp.dot(att[:, :split], wo[c, :split], preferred_element_type=F32)
        proj[2 * c] = acc[:, :HD]
        proj[2 * c + 1] = acc[:, HD:]

    collect(1, EARLY, HEADS)
    for c in range(NCHUNK):
        columns = slice(c * CHUNK, (c + 1) * CHUNK)
        early = jnp.concatenate([proj[2 * c], proj[2 * c + 1]], axis=1)
        out_ref[:, columns] = (
            (early + jnp.dot(att[:, split:], wo[c, split:], preferred_element_type=F32)) * mod_ref[2:3, columns]
        ).astype(BF16)

    @pl.loop(0, HEADS)
    def _(h):
        flow(own_wd, h).wait_send()
        flow(own_sib, h).wait_send()
        flow(wd_sib, h).wait_send()

        @pl.when(inner)
        def _():
            flow(own_ac, h).wait_send()
            flow(wd_ac, h).wait_send()

        turn, ac_turn = turned(h), ac_turned(h)
        pl.when(jnp.logical_and(has_to, jnp.logical_not(turn)))(lambda: flow(wd_to, h).wait_send())
        pl.when(jnp.logical_and(inner_to, jnp.logical_not(ac_turn)))(lambda: flow(ac_to, h).wait_send())
        pl.when(jnp.logical_and(has_from, in_transit(h)))(lambda: turn_flow(0, h).wait_send())
        pl.when(jnp.logical_and(has_to, turn))(lambda: turn_flow(1, h).wait_send())
        pl.when(jnp.logical_and(inner_to, ac_turn))(lambda: turn_flow(2, h).wait_send())
        pl.when(has_from)(lambda: flow(wz_sib, h).wait_send())

        @pl.when(has_next)
        def _():
            query_flow(0, h).wait_send()
            result_flow(1, h).wait_send()

        @pl.when(has_prev)
        def _():
            query_flow(1, h).wait_send()
            result_flow(0, h).wait_send()

    for stage in range(2):
        pl.when(has_prev)(lambda: stat_flow(stage, 0).wait_send())
        pl.when(has_next)(lambda: stat_flow(stage, 1).wait_send())


def body(tokens, modulation, w_query, w_key, w_value, w_out, norm_q, norm_k):
    vmem = pl.BlockSpec(memory_space=pltpu.VMEM)
    hbm = pl.BlockSpec(memory_space=pl.ANY)
    weight = pltpu.VMEM((NCHUNK, D, CHUNK), BF16)
    dma = pltpu.SemaphoreType.DMA
    result = pl.pallas_call(
        kernel,
        out_shape=jax.ShapeDtypeStruct((N, D), BF16),
        in_specs=[vmem] * 5 + [hbm] * 4,
        out_specs=vmem,
        scratch_shapes=[
            weight, weight, weight, weight,
            pltpu.VMEM((N, D), BF16),
            pltpu.VMEM((HEADS, N, HD), F32),
            pltpu.VMEM((N, 3 * HD), F32),
            pltpu.VMEM((SLOTS, HEADS, N, 2 * HD), BF16),
            pltpu.VMEM(((HEADS - AC_TURN) // 2, N, 2 * HD), BF16),
            pltpu.VMEM((SLOTS, N, HD), BF16),
            pltpu.VMEM((3, HEADS, N, HD), BF16),
            pltpu.VMEM((2, HEADS, N, HD), BF16),
            pltpu.VMEM((2, HEADS, N, HD), BF16),
            pltpu.VMEM((HEADS, N, HD), F32),
            pltpu.VMEM((2, 2, 16, 256), F32),
            pltpu.VMEM((2, 2, 16, 256), F32),
            pltpu.VMEM((3, 256, HD), F32),
            pltpu.VMEM((N, D), BF16),
            dma((4, NCHUNK)),
            dma((8, HEADS)), dma((8, HEADS)),
            dma((3, (HEADS - AC_TURN) // 2)), dma((3, (HEADS - AC_TURN) // 2)),
            dma((2, HEADS)), dma((2, HEADS)),
            dma((2, HEADS)), dma((2, HEADS)),
            dma((2, 2)), dma((2, 2)),
        ],
        compiler_params=pltpu.CompilerParams(
            collective_id=0, has_side_effects=True, vmem_limit_bytes=60 * 1024 * 1024
        ),
        name="tile_attention",
    )(
        tokens.reshape(N, D),
        modulation,
        norm_q,
        norm_k,
        jnp.asarray(angle_tables()),
        w_query, w_key, w_value, w_out,
    )
    return result.reshape(3, 8, 8, D)


def solution(mesh):
    in_specs = (P("ta", "ha", "wa", None), P(), P(), P(), P(), P(), P(), P())
    out_specs = P("ta", "ha", "wa", None)
    return jax.shard_map(body, mesh=mesh, in_specs=in_specs, out_specs=out_specs, check_vma=False)
```

```python
import jax
import jax.numpy as jnp
import numpy as np
from jax import lax
from jax.experimental import pallas as pl
from jax.experimental.pallas import tpu as pltpu
from jax.sharding import PartitionSpec as P

HEADS = 12
HD = 128
D = 1536
N = 192
CHUNK = 256
NCHUNK = D // CHUNK
SLOTS = 9
OWN, WD, WZ, SIB, SIB_WD, SIB_WZ, AC_WD, AC, AC_WZ = range(SLOTS)
AHEAD = 3
SHARE = 1
AT_ONCE = 6
TURN = 8
AC_TURN = 0
EARLY = 10
MESH = pl.DeviceIdType.MESH
F32 = jnp.float32
BF16 = jnp.bfloat16


def angle_tables():
    half, sixth = HD // 2, HD // 6
    first = half - 2 * sixth
    freq_first = 10000.0 ** (-np.arange(first) / first)
    freq_rest = 10000.0 ** (-np.arange(sixth) / sixth)
    table = np.zeros((16, 8, 3, HD))
    for base, groups, size, start, freq in (
        (0, 4, 3, 0, freq_first),
        (4, 4, 8, first, freq_rest),
        (8, 8, 8, first + sixth, freq_rest),
    ):
        for group in range(groups):
            for row in range(size):
                angle = (group * size + row) * freq
                lanes = 2 * (start + np.arange(len(freq)))
                table[base + group, row, 0, lanes] = np.cos(angle)
                table[base + group, row, 0, lanes + 1] = np.cos(angle)
                table[base + group, row, 1, lanes] = -np.sin(angle)
                table[base + group, row, 2, lanes + 1] = np.sin(angle)
    return table.reshape(16, 8, 3 * HD).astype(np.float32)


def kernel(
    tok_ref, mod_ref, nq_ref, nk_ref, tab_ref, wq_hbm, wk_hbm, wv_hbm, wo_hbm,
    out_ref,
    wq, wk, wv, wo, xn, proj, cs, kv, transit, ones, q, o_send, o_recv, o_own, st_send, st_recv, st_parts, att,
    w_sem, kv_send, kv_recv, tr_send, tr_recv, q_send, q_recv, o_ssem, o_rsem, st_ssem, st_rsem,
):
    ta, ha, wa = lax.axis_index("ta"), lax.axis_index("ha"), lax.axis_index("wa")
    edge = lax.rem(wa, 2)
    step = 2 - 4 * edge
    z_to, z_from = wa + step, wa - step
    has_to = jnp.logical_and(z_to >= 0, z_to < 8)
    has_from = jnp.logical_and(z_from >= 0, z_from < 8)
    inner = jnp.logical_and(ha >= 1, ha <= 2)
    inner_to = jnp.logical_and(inner, has_to)
    inner_from = jnp.logical_and(inner, has_from)
    has_prev, has_next = ta > 0, ta < 3
    direct = wa + 1 - 2 * edge
    sib = ha + 1 - 2 * lax.rem(ha, 2)
    dev_wd = (ta, ha, direct)
    dev_sib = (ta, sib, wa)
    dev_ac = (ta, 3 - ha, direct)
    dev_to = (ta, ha, z_to)
    dev_from = (ta, ha, z_from)
    dev_prev = (ta - 1, ha, wa)
    dev_next = (ta + 1, ha, wa)

    weights = ((wk_hbm, wk), (wv_hbm, wv), (wq_hbm, wq), (wo_hbm, wo))

    def weight_copy(which, c):
        hbm, buf = weights[which]
        return pltpu.make_async_copy(
            hbm.at[:, pl.ds(pl.multiple_of(c * CHUNK, CHUNK), CHUNK)], buf.at[c], w_sem.at[which, c]
        )

    for which in range(4):
        for c in range(NCHUNK):
            weight_copy(which, c).start()

    barrier = pltpu.get_barrier_semaphore()

    def greet(device):
        pl.semaphore_signal(barrier, inc=1, device_id=device, device_id_type=MESH)

    greet(dev_wd)
    greet(dev_sib)
    pl.when(has_to)(lambda: greet(dev_to))
    pl.when(has_from)(lambda: greet(dev_from))
    pl.when(inner)(lambda: greet(dev_ac))
    pl.when(has_prev)(lambda: greet(dev_prev))
    pl.when(has_next)(lambda: greet(dev_next))

    tf, tr, tc = tab_ref[ta], tab_ref[4 + ha], tab_ref[8 + wa]
    for f in range(3):
        for r in range(8):
            cs[pl.ds((f * 8 + r) * 8, 8), :] = tc + tr[r : r + 1, :] + tf[f : f + 1, :]

    scale = 1.0 + mod_ref[1:2, :]
    shift = mod_ref[0:1, :]
    for r in range(N // 32):
        rows = pl.ds(r * 32, 32)
        values = tok_ref[rows, :].astype(F32)
        center = values - jnp.mean(values, axis=-1, keepdims=True)
        spread = jnp.mean(center * center, axis=-1, keepdims=True)
        xn[rows, :] = (center * lax.rsqrt(spread + 1e-6) * scale + shift).astype(BF16)

    def project(which, store):
        def one(c, total):
            weight_copy(which, c).wait()
            acc = jnp.dot(xn[...], weights[which][1][c], preferred_element_type=F32)
            return store(c, acc, total)

        return lax.fori_loop(0, NCHUNK, one, jnp.zeros((N, HD), F32))

    def keep(c, acc, total):
        left, right = acc[:, :HD], acc[:, HD:]
        proj[2 * c] = left
        proj[2 * c + 1] = right
        return total + left * left + right * right

    def rotated(h, inv, gain_ref):
        x = proj[h] * inv * gain_ref[pl.ds(pl.multiple_of(h * HD, HD), HD)].reshape(1, HD)
        return (
            x * cs[:, :HD]
            + pltpu.roll(x, HD - 1, 1) * cs[:, HD : 2 * HD]
            + pltpu.roll(x, 1, 1) * cs[:, 2 * HD :]
        ).astype(BF16)

    def inverse(total):
        return lax.rsqrt(jnp.sum(total, axis=-1, keepdims=True) * (1.0 / D) + 1e-6)

    own_wd = (0, OWN, WD, dev_wd)
    own_sib = (1, OWN, SIB, dev_sib)
    own_ac = (2, OWN, AC_WD, dev_ac)
    wd_to = (3, WD, WZ, dev_to)
    wd_sib = (4, WD, SIB_WD, dev_sib)
    wd_ac = (5, WD, AC, dev_ac)
    ac_to = (6, AC_WD, AC_WZ, dev_to)
    wz_sib = (7, WZ, SIB_WZ, dev_sib)

    def flow(which, h):
        index, source, target, device = which
        return pltpu.make_async_remote_copy(
            src_ref=kv.at[source, h],
            dst_ref=kv.at[target, h],
            send_sem=kv_send.at[index, h],
            recv_sem=kv_recv.at[index, h],
            device_id=device,
            device_id_type=MESH,
        )

    def turned(h):
        return jnp.logical_and(h >= TURN, h % 2 == 0)

    def ac_turned(h):
        return jnp.logical_and(h >= AC_TURN, h % 2 == 0)

    def in_transit(h):
        return jnp.logical_or(turned(h), jnp.logical_and(inner, ac_turned(h)))

    def turn_flow(leg, h):
        k = (h - AC_TURN) // 2
        source = kv.at[OWN, h] if leg == 0 else transit.at[k]
        target = (transit.at[k], kv.at[WZ, h], kv.at[AC_WZ, h])[leg]
        return pltpu.make_async_remote_copy(
            src_ref=source,
            dst_ref=target,
            send_sem=tr_send.at[leg, k],
            recv_sem=tr_recv.at[leg, k],
            device_id=(dev_from, dev_wd, dev_ac)[leg],
            device_id_type=MESH,
        )

    inv_k = inverse(project(0, keep))

    partners = (
        2
        + has_to.astype(jnp.int32)
        + has_from.astype(jnp.int32)
        + inner.astype(jnp.int32)
        + has_prev.astype(jnp.int32)
        + has_next.astype(jnp.int32)
    )
    pl.semaphore_wait(barrier, partners)

    def store_and_send(c, acc, total):
        for half in range(2):
            h = 2 * c + half
            kv[OWN, h, :, HD:] = acc[:, half * HD : (half + 1) * HD].astype(BF16)
            kv[OWN, h, :, :HD] = rotated(h, inv_k, nk_ref)
            flow(own_wd, h).start()
            pl.when(jnp.logical_and(inner, h < AT_ONCE))(lambda: flow(own_ac, h).start())
            flow(own_sib, h).start()
            pl.when(jnp.logical_and(has_from, in_transit(h)))(lambda: turn_flow(0, h).start())
        return total

    project(1, store_and_send)

    def absent(slot):
        ones[slot] = jnp.zeros((N, HD), BF16)

        @pl.loop(0, HEADS)
        def _(h):
            kv[slot, h, :, :HD] = kv[OWN, h, :, :HD]
            kv[slot, h, :, HD:] = jnp.zeros((N, HD), BF16)

    for slot in range(SLOTS):
        ones[slot] = jnp.ones((N, HD), BF16)

    @pl.when(jnp.logical_not(has_from))
    def _():
        absent(WZ)
        absent(SIB_WZ)

    @pl.when(jnp.logical_and(inner, jnp.logical_not(has_from)))
    def _():
        absent(AC_WZ)

    @pl.when(jnp.logical_not(has_prev))
    def _():
        q[1] = jnp.zeros((HEADS, N, HD), BF16)
        o_recv[0] = jnp.zeros((HEADS, N, HD), BF16)
        st_recv[:, 0] = jnp.full((2, 16, 256), -1e30, F32)

    @pl.when(jnp.logical_not(has_next))
    def _():
        q[2] = jnp.zeros((HEADS, N, HD), BF16)
        o_recv[1] = jnp.zeros((HEADS, N, HD), BF16)
        st_recv[:, 1] = jnp.full((2, 16, 256), -1e30, F32)

    def query_flow(which, h):
        return pltpu.make_async_remote_copy(
            src_ref=q.at[0, h],
            dst_ref=q.at[1 + which, h],
            send_sem=q_send.at[which, h],
            recv_sem=q_recv.at[which, h],
            device_id=(dev_next, dev_prev)[which],
            device_id_type=MESH,
        )

    def result_flow(which, h):
        return pltpu.make_async_remote_copy(
            src_ref=o_send.at[which, h],
            dst_ref=o_recv.at[1 - which, h],
            send_sem=o_ssem.at[which, h],
            recv_sem=o_rsem.at[1 - which, h],
            device_id=(dev_prev, dev_next)[which],
            device_id_type=MESH,
        )

    def stat_flow(stage, which):
        return pltpu.make_async_remote_copy(
            src_ref=st_send.at[stage, which],
            dst_ref=st_recv.at[stage, 1 - which],
            send_sem=st_ssem.at[stage, which],
            recv_sem=st_rsem.at[stage, 1 - which],
            device_id=(dev_prev, dev_next)[which],
            device_id_type=MESH,
        )

    def pass_on(h):
        flow(own_wd, h).wait_recv()
        turn, ac_turn = turned(h), ac_turned(h)
        pl.when(jnp.logical_and(has_to, jnp.logical_not(turn)))(lambda: flow(wd_to, h).start())
        pl.when(jnp.logical_and(inner, h + AT_ONCE < HEADS))(lambda: flow(own_ac, h + AT_ONCE).start())
        pl.when(inner)(lambda: flow(wd_ac, h).start())
        flow(wd_sib, h).start()
        pl.when(inner)(lambda: flow(own_ac, h).wait_recv())
        pl.when(jnp.logical_and(inner_to, jnp.logical_not(ac_turn)))(lambda: flow(ac_to, h).start())

        @pl.when(jnp.logical_and(has_to, in_transit(h)))
        def _():
            turn_flow(0, h).wait_recv()
            pl.when(turn)(lambda: turn_flow(1, h).start())
            pl.when(jnp.logical_and(inner, ac_turn))(lambda: turn_flow(2, h).start())

    def share(h):
        turn = turned(h)

        @pl.when(has_from)
        def _():
            pl.when(jnp.logical_not(turn))(lambda: flow(wd_to, h).wait_recv())
            pl.when(turn)(lambda: turn_flow(1, h).wait_recv())
            flow(wz_sib, h).start()

    inv_q = inverse(project(2, keep))
    pass_on(0)

    @pl.loop(0, HEADS // 2)
    def _(h):
        q[0, h] = rotated(h, inv_q, nq_ref)
        pl.when(has_next)(lambda: query_flow(0, h).start())
        pl.when(has_prev)(lambda: query_flow(1, h).start())

    pass_on(1)

    @pl.loop(HEADS // 2, HEADS)
    def _(h):
        q[0, h] = rotated(h, inv_q, nq_ref)
        pl.when(has_next)(lambda: query_flow(0, h).start())
        pl.when(has_prev)(lambda: query_flow(1, h).start())

    for h in range(2, AHEAD):
        pass_on(h)
    for h in range(SHARE):
        share(h)

    factor = HD ** (-0.5) * float(np.log2(np.e))
    lanes = lax.broadcasted_iota(jnp.int32, (N, HD), 1)
    st_parts[...] = jnp.zeros((3, 256, HD), F32)

    def send_stats(stage):
        for which, has in ((0, has_prev), (1, has_next)):
            st_send[stage, which] = jnp.transpose(st_parts[1 + which])[:16]
            pl.when(has)(lambda: stat_flow(stage, which).start())

    @pl.loop(0, HEADS)
    def _(h):
        ahead = AHEAD + h + h // 2
        pl.when(ahead < HEADS)(lambda: pass_on(ahead))
        ac_turn = ac_turned(h)
        flow(own_sib, h).wait_recv()
        flow(wd_sib, h).wait_recv()
        pl.when(inner)(lambda: flow(wd_ac, h).wait_recv())
        pl.when(jnp.logical_and(inner_from, jnp.logical_not(ac_turn)))(lambda: flow(ac_to, h).wait_recv())
        pl.when(jnp.logical_and(inner_from, ac_turn))(lambda: turn_flow(2, h).wait_recv())
        pl.when(has_from)(lambda: flow(wz_sib, h).wait_recv())
        pl.when(has_prev)(lambda: query_flow(0, h).wait_recv())
        pl.when(has_next)(lambda: query_flow(1, h).wait_recv())

        def attend(part, slots):
            keys = kv[:slots, h, :, :HD].reshape(slots * N, HD)
            values = jnp.concatenate(
                [kv[:slots, h, :, HD:].reshape(slots * N, HD), ones[:slots].reshape(slots * N, HD)], axis=1
            )
            scores = lax.dot_general(
                q[part, h], keys, (((1,), (1,)), ((), ())), preferred_element_type=F32
            )
            peak = jnp.max(scores, axis=-1, keepdims=True)
            expo = jnp.exp2((scores - peak) * factor).astype(BF16)
            acc = jnp.dot(expo, values, preferred_element_type=F32)
            stat = peak * factor + jnp.log2(acc[:, HD:])
            st_parts[part, :N] = jnp.where(lanes == h, stat, st_parts[part, :N])
            return acc[:, :HD] / acc[:, HD:]

        def other_frames(slots):
            for part in (1, 2):
                o_send[part - 1, h] = attend(part, slots).astype(BF16)

        def own_frames(slots):
            o_own[h] = attend(0, slots)

        pl.when(inner)(lambda: other_frames(SLOTS))
        pl.when(jnp.logical_not(inner))(lambda: other_frames(AC_WD))
        pl.when(has_prev)(lambda: result_flow(0, h).start())
        pl.when(has_next)(lambda: result_flow(1, h).start())
        pl.when(h + SHARE < HEADS)(lambda: share(h + SHARE))
        pl.when(jnp.logical_and(h % 2 == 1, ahead + 1 < HEADS))(lambda: pass_on(ahead + 1))
        pl.when(inner)(lambda: own_frames(SLOTS))
        pl.when(jnp.logical_not(inner))(lambda: own_frames(AC_WD))

        pl.when(h == EARLY - 1)(lambda: send_stats(0))

    send_stats(1)

    def collect(stage, first, last):
        for which, has in ((0, has_next), (1, has_prev)):

            @pl.when(has)
            def _():
                stat_flow(stage, which).wait_recv()

                @pl.loop(first, last)
                def _(h):
                    result_flow(which, h).wait_recv()

        below = jnp.zeros((HD - 16, 256), F32)
        l_prev = jnp.transpose(jnp.concatenate([st_recv[stage, 0], below], axis=0))[:N]
        l_next = jnp.transpose(jnp.concatenate([st_recv[stage, 1], below], axis=0))[:N]
        l_own = st_parts[0, :N]
        top = jnp.maximum(jnp.maximum(l_prev, l_next), l_own)
        e_prev, e_next, e_own = jnp.exp2(l_prev - top), jnp.exp2(l_next - top), jnp.exp2(l_own - top)
        total = 1.0 / (e_prev + e_next + e_own)
        e_prev, e_next, e_own = e_prev * total, e_next * total, e_own * total
        for h in range(first, last):
            column = slice(h, h + 1)
            att[:, h * HD : (h + 1) * HD] = (
                e_own[:, column] * o_own[h]
                + e_prev[:, column] * o_recv[0, h].astype(F32)
                + e_next[:, column] * o_recv[1, h].astype(F32)
            ).astype(BF16)

    split = EARLY * HD
    collect(0, 0, EARLY)
    for c in range(NCHUNK):
        weight_copy(3, c).wait()
        acc = jnp.dot(att[:, :split], wo[c, :split], preferred_element_type=F32)
        proj[2 * c] = acc[:, :HD]
        proj[2 * c + 1] = acc[:, HD:]

    collect(1, EARLY, HEADS)
    for c in range(NCHUNK):
        columns = slice(c * CHUNK, (c + 1) * CHUNK)
        early = jnp.concatenate([proj[2 * c], proj[2 * c + 1]], axis=1)
        out_ref[:, columns] = (
            (early + jnp.dot(att[:, split:], wo[c, split:], preferred_element_type=F32)) * mod_ref[2:3, columns]
        ).astype(BF16)

    @pl.loop(0, HEADS)
    def _(h):
        flow(own_wd, h).wait_send()
        flow(own_sib, h).wait_send()
        flow(wd_sib, h).wait_send()

        @pl.when(inner)
        def _():
            flow(own_ac, h).wait_send()
            flow(wd_ac, h).wait_send()

        turn, ac_turn = turned(h), ac_turned(h)
        pl.when(jnp.logical_and(has_to, jnp.logical_not(turn)))(lambda: flow(wd_to, h).wait_send())
        pl.when(jnp.logical_and(inner_to, jnp.logical_not(ac_turn)))(lambda: flow(ac_to, h).wait_send())
        pl.when(jnp.logical_and(has_from, in_transit(h)))(lambda: turn_flow(0, h).wait_send())
        pl.when(jnp.logical_and(has_to, turn))(lambda: turn_flow(1, h).wait_send())
        pl.when(jnp.logical_and(inner_to, ac_turn))(lambda: turn_flow(2, h).wait_send())
        pl.when(has_from)(lambda: flow(wz_sib, h).wait_send())

        @pl.when(has_next)
        def _():
            query_flow(0, h).wait_send()
            result_flow(1, h).wait_send()

        @pl.when(has_prev)
        def _():
            query_flow(1, h).wait_send()
            result_flow(0, h).wait_send()

    for stage in range(2):
        pl.when(has_prev)(lambda: stat_flow(stage, 0).wait_send())
        pl.when(has_next)(lambda: stat_flow(stage, 1).wait_send())


def body(tokens, modulation, w_query, w_key, w_value, w_out, norm_q, norm_k):
    vmem = pl.BlockSpec(memory_space=pltpu.VMEM)
    hbm = pl.BlockSpec(memory_space=pl.ANY)
    weight = pltpu.VMEM((NCHUNK, D, CHUNK), BF16)
    dma = pltpu.SemaphoreType.DMA
    result = pl.pallas_call(
        kernel,
        out_shape=jax.ShapeDtypeStruct((N, D), BF16),
        in_specs=[vmem] * 5 + [hbm] * 4,
        out_specs=vmem,
        scratch_shapes=[
            weight, weight, weight, weight,
            pltpu.VMEM((N, D), BF16),
            pltpu.VMEM((HEADS, N, HD), F32),
            pltpu.VMEM((N, 3 * HD), F32),
            pltpu.VMEM((SLOTS, HEADS, N, 2 * HD), BF16),
            pltpu.VMEM(((HEADS - AC_TURN) // 2, N, 2 * HD), BF16),
            pltpu.VMEM((SLOTS, N, HD), BF16),
            pltpu.VMEM((3, HEADS, N, HD), BF16),
            pltpu.VMEM((2, HEADS, N, HD), BF16),
            pltpu.VMEM((2, HEADS, N, HD), BF16),
            pltpu.VMEM((HEADS, N, HD), F32),
            pltpu.VMEM((2, 2, 16, 256), F32),
            pltpu.VMEM((2, 2, 16, 256), F32),
            pltpu.VMEM((3, 256, HD), F32),
            pltpu.VMEM((N, D), BF16),
            dma((4, NCHUNK)),
            dma((8, HEADS)), dma((8, HEADS)),
            dma((3, (HEADS - AC_TURN) // 2)), dma((3, (HEADS - AC_TURN) // 2)),
            dma((2, HEADS)), dma((2, HEADS)),
            dma((2, HEADS)), dma((2, HEADS)),
            dma((2, 2)), dma((2, 2)),
        ],
        compiler_params=pltpu.CompilerParams(
            collective_id=0, has_side_effects=True, vmem_limit_bytes=60 * 1024 * 1024
        ),
        name="tile_attention",
    )(
        tokens.reshape(N, D),
        modulation,
        norm_q,
        norm_k,
        jnp.asarray(angle_tables()),
        w_query, w_key, w_value, w_out,
    )
    return result.reshape(3, 8, 8, D)


def solution(mesh):
    in_specs = (P("ta", "ha", "wa", None), P(), P(), P(), P(), P(), P(), P())
    out_specs = P("ta", "ha", "wa", None)
    return jax.shard_map(body, mesh=mesh, in_specs=in_specs, out_specs=out_specs, check_vma=False)
```

```python
import jax
import jax.numpy as jnp
import numpy as np
from jax import lax
from jax.experimental import pallas as pl
from jax.experimental.pallas import tpu as pltpu
from jax.sharding import PartitionSpec as P

HEADS = 12
HD = 128
D = 1536
N = 192
CHUNK = 256
NCHUNK = D // CHUNK
SLOTS = 9
OWN, WD, WZ, SIB, SIB_WD, SIB_WZ, AC_WD, AC, AC_WZ = range(SLOTS)
AHEAD = 3
SHARE = 1
AT_ONCE = 8
TURN = 8
AC_TURN = 0
EARLY = 10
MESH = pl.DeviceIdType.MESH
F32 = jnp.float32
BF16 = jnp.bfloat16


def angle_tables():
    half, sixth = HD // 2, HD // 6
    first = half - 2 * sixth
    freq_first = 10000.0 ** (-np.arange(first) / first)
    freq_rest = 10000.0 ** (-np.arange(sixth) / sixth)
    table = np.zeros((16, 8, 3, HD))
    for base, groups, size, start, freq in (
        (0, 4, 3, 0, freq_first),
        (4, 4, 8, first, freq_rest),
        (8, 8, 8, first + sixth, freq_rest),
    ):
        for group in range(groups):
            for row in range(size):
                angle = (group * size + row) * freq
                lanes = 2 * (start + np.arange(len(freq)))
                table[base + group, row, 0, lanes] = np.cos(angle)
                table[base + group, row, 0, lanes + 1] = np.cos(angle)
                table[base + group, row, 1, lanes] = -np.sin(angle)
                table[base + group, row, 2, lanes + 1] = np.sin(angle)
    return table.reshape(16, 8, 3 * HD).astype(np.float32)


def kernel(
    tok_ref, mod_ref, nq_ref, nk_ref, tab_ref, wq_hbm, wk_hbm, wv_hbm, wo_hbm,
    out_ref,
    wq, wk, wv, wo, xn, proj, cs, kv, transit, ones, q, o_send, o_recv, o_own, st_send, st_recv, st_parts, att,
    w_sem, kv_send, kv_recv, tr_send, tr_recv, q_send, q_recv, o_ssem, o_rsem, st_ssem, st_rsem,
):
    ta, ha, wa = lax.axis_index("ta"), lax.axis_index("ha"), lax.axis_index("wa")
    edge = lax.rem(wa, 2)
    step = 2 - 4 * edge
    z_to, z_from = wa + step, wa - step
    has_to = jnp.logical_and(z_to >= 0, z_to < 8)
    has_from = jnp.logical_and(z_from >= 0, z_from < 8)
    inner = jnp.logical_and(ha >= 1, ha <= 2)
    inner_to = jnp.logical_and(inner, has_to)
    inner_from = jnp.logical_and(inner, has_from)
    has_prev, has_next = ta > 0, ta < 3
    direct = wa + 1 - 2 * edge
    sib = ha + 1 - 2 * lax.rem(ha, 2)
    dev_wd = (ta, ha, direct)
    dev_sib = (ta, sib, wa)
    dev_ac = (ta, 3 - ha, direct)
    dev_to = (ta, ha, z_to)
    dev_from = (ta, ha, z_from)
    dev_prev = (ta - 1, ha, wa)
    dev_next = (ta + 1, ha, wa)

    weights = ((wk_hbm, wk), (wv_hbm, wv), (wq_hbm, wq), (wo_hbm, wo))

    def weight_copy(which, c):
        hbm, buf = weights[which]
        return pltpu.make_async_copy(
            hbm.at[:, pl.ds(pl.multiple_of(c * CHUNK, CHUNK), CHUNK)], buf.at[c], w_sem.at[which, c]
        )

    for which in range(4):
        for c in range(NCHUNK):
            weight_copy(which, c).start()

    barrier = pltpu.get_barrier_semaphore()

    def greet(device):
        pl.semaphore_signal(barrier, inc=1, device_id=device, device_id_type=MESH)

    greet(dev_wd)
    greet(dev_sib)
    pl.when(has_to)(lambda: greet(dev_to))
    pl.when(has_from)(lambda: greet(dev_from))
    pl.when(inner)(lambda: greet(dev_ac))
    pl.when(has_prev)(lambda: greet(dev_prev))
    pl.when(has_next)(lambda: greet(dev_next))

    tf, tr, tc = tab_ref[ta], tab_ref[4 + ha], tab_ref[8 + wa]
    for f in range(3):
        for r in range(8):
            cs[pl.ds((f * 8 + r) * 8, 8), :] = tc + tr[r : r + 1, :] + tf[f : f + 1, :]

    scale = 1.0 + mod_ref[1:2, :]
    shift = mod_ref[0:1, :]
    for r in range(N // 32):
        rows = pl.ds(r * 32, 32)
        values = tok_ref[rows, :].astype(F32)
        center = values - jnp.mean(values, axis=-1, keepdims=True)
        spread = jnp.mean(center * center, axis=-1, keepdims=True)
        xn[rows, :] = (center * lax.rsqrt(spread + 1e-6) * scale + shift).astype(BF16)

    def project(which, store):
        def one(c, total):
            weight_copy(which, c).wait()
            acc = jnp.dot(xn[...], weights[which][1][c], preferred_element_type=F32)
            return store(c, acc, total)

        return lax.fori_loop(0, NCHUNK, one, jnp.zeros((N, HD), F32))

    def keep(c, acc, total):
        left, right = acc[:, :HD], acc[:, HD:]
        proj[2 * c] = left
        proj[2 * c + 1] = right
        return total + left * left + right * right

    def rotated(h, inv, gain_ref):
        x = proj[h] * inv * gain_ref[pl.ds(pl.multiple_of(h * HD, HD), HD)].reshape(1, HD)
        return (
            x * cs[:, :HD]
            + pltpu.roll(x, HD - 1, 1) * cs[:, HD : 2 * HD]
            + pltpu.roll(x, 1, 1) * cs[:, 2 * HD :]
        ).astype(BF16)

    def inverse(total):
        return lax.rsqrt(jnp.sum(total, axis=-1, keepdims=True) * (1.0 / D) + 1e-6)

    own_wd = (0, OWN, WD, dev_wd)
    own_sib = (1, OWN, SIB, dev_sib)
    own_ac = (2, OWN, AC_WD, dev_ac)
    wd_to = (3, WD, WZ, dev_to)
    wd_sib = (4, WD, SIB_WD, dev_sib)
    wd_ac = (5, WD, AC, dev_ac)
    ac_to = (6, AC_WD, AC_WZ, dev_to)
    wz_sib = (7, WZ, SIB_WZ, dev_sib)

    def flow(which, h):
        index, source, target, device = which
        return pltpu.make_async_remote_copy(
            src_ref=kv.at[source, h],
            dst_ref=kv.at[target, h],
            send_sem=kv_send.at[index, h],
            recv_sem=kv_recv.at[index, h],
            device_id=device,
            device_id_type=MESH,
        )

    def turned(h):
        return jnp.logical_and(h >= TURN, h % 2 == 0)

    def ac_turned(h):
        return jnp.logical_and(h >= AC_TURN, h % 2 == 0)

    def in_transit(h):
        return jnp.logical_or(turned(h), jnp.logical_and(inner, ac_turned(h)))

    def turn_flow(leg, h):
        k = (h - AC_TURN) // 2
        source = kv.at[OWN, h] if leg == 0 else transit.at[k]
        target = (transit.at[k], kv.at[WZ, h], kv.at[AC_WZ, h])[leg]
        return pltpu.make_async_remote_copy(
            src_ref=source,
            dst_ref=target,
            send_sem=tr_send.at[leg, k],
            recv_sem=tr_recv.at[leg, k],
            device_id=(dev_from, dev_wd, dev_ac)[leg],
            device_id_type=MESH,
        )

    inv_k = inverse(project(0, keep))

    partners = (
        2
        + has_to.astype(jnp.int32)
        + has_from.astype(jnp.int32)
        + inner.astype(jnp.int32)
        + has_prev.astype(jnp.int32)
        + has_next.astype(jnp.int32)
    )
    pl.semaphore_wait(barrier, partners)

    def store_and_send(c, acc, total):
        for half in range(2):
            h = 2 * c + half
            kv[OWN, h, :, HD:] = acc[:, half * HD : (half + 1) * HD].astype(BF16)
            kv[OWN, h, :, :HD] = rotated(h, inv_k, nk_ref)
            flow(own_wd, h).start()
            pl.when(jnp.logical_and(inner, h < AT_ONCE))(lambda: flow(own_ac, h).start())
            flow(own_sib, h).start()
            pl.when(jnp.logical_and(has_from, in_transit(h)))(lambda: turn_flow(0, h).start())
        return total

    project(1, store_and_send)

    def absent(slot):
        ones[slot] = jnp.zeros((N, HD), BF16)

        @pl.loop(0, HEADS)
        def _(h):
            kv[slot, h, :, :HD] = kv[OWN, h, :, :HD]
            kv[slot, h, :, HD:] = jnp.zeros((N, HD), BF16)

    for slot in range(SLOTS):
        ones[slot] = jnp.ones((N, HD), BF16)

    @pl.when(jnp.logical_not(has_from))
    def _():
        absent(WZ)
        absent(SIB_WZ)

    @pl.when(jnp.logical_and(inner, jnp.logical_not(has_from)))
    def _():
        absent(AC_WZ)

    @pl.when(jnp.logical_not(has_prev))
    def _():
        q[1] = jnp.zeros((HEADS, N, HD), BF16)
        o_recv[0] = jnp.zeros((HEADS, N, HD), BF16)
        st_recv[:, 0] = jnp.full((2, 16, 256), -1e30, F32)

    @pl.when(jnp.logical_not(has_next))
    def _():
        q[2] = jnp.zeros((HEADS, N, HD), BF16)
        o_recv[1] = jnp.zeros((HEADS, N, HD), BF16)
        st_recv[:, 1] = jnp.full((2, 16, 256), -1e30, F32)

    def query_flow(which, h):
        return pltpu.make_async_remote_copy(
            src_ref=q.at[0, h],
            dst_ref=q.at[1 + which, h],
            send_sem=q_send.at[which, h],
            recv_sem=q_recv.at[which, h],
            device_id=(dev_next, dev_prev)[which],
            device_id_type=MESH,
        )

    def result_flow(which, h):
        return pltpu.make_async_remote_copy(
            src_ref=o_send.at[which, h],
            dst_ref=o_recv.at[1 - which, h],
            send_sem=o_ssem.at[which, h],
            recv_sem=o_rsem.at[1 - which, h],
            device_id=(dev_prev, dev_next)[which],
            device_id_type=MESH,
        )

    def stat_flow(stage, which):
        return pltpu.make_async_remote_copy(
            src_ref=st_send.at[stage, which],
            dst_ref=st_recv.at[stage, 1 - which],
            send_sem=st_ssem.at[stage, which],
            recv_sem=st_rsem.at[stage, 1 - which],
            device_id=(dev_prev, dev_next)[which],
            device_id_type=MESH,
        )

    def pass_on(h):
        flow(own_wd, h).wait_recv()
        turn, ac_turn = turned(h), ac_turned(h)
        pl.when(jnp.logical_and(has_to, jnp.logical_not(turn)))(lambda: flow(wd_to, h).start())
        pl.when(jnp.logical_and(inner, h + AT_ONCE < HEADS))(lambda: flow(own_ac, h + AT_ONCE).start())
        pl.when(inner)(lambda: flow(wd_ac, h).start())
        flow(wd_sib, h).start()
        pl.when(inner)(lambda: flow(own_ac, h).wait_recv())
        pl.when(jnp.logical_and(inner_to, jnp.logical_not(ac_turn)))(lambda: flow(ac_to, h).start())

        @pl.when(jnp.logical_and(has_to, in_transit(h)))
        def _():
            turn_flow(0, h).wait_recv()
            pl.when(turn)(lambda: turn_flow(1, h).start())
            pl.when(jnp.logical_and(inner, ac_turn))(lambda: turn_flow(2, h).start())

    def share(h):
        turn = turned(h)

        @pl.when(has_from)
        def _():
            pl.when(jnp.logical_not(turn))(lambda: flow(wd_to, h).wait_recv())
            pl.when(turn)(lambda: turn_flow(1, h).wait_recv())
            flow(wz_sib, h).start()

    inv_q = inverse(project(2, keep))
    pass_on(0)

    @pl.loop(0, HEADS // 2)
    def _(h):
        q[0, h] = rotated(h, inv_q, nq_ref)
        pl.when(has_next)(lambda: query_flow(0, h).start())
        pl.when(has_prev)(lambda: query_flow(1, h).start())

    pass_on(1)

    @pl.loop(HEADS // 2, HEADS)
    def _(h):
        q[0, h] = rotated(h, inv_q, nq_ref)
        pl.when(has_next)(lambda: query_flow(0, h).start())
        pl.when(has_prev)(lambda: query_flow(1, h).start())

    for h in range(2, AHEAD):
        pass_on(h)
    for h in range(SHARE):
        share(h)

    factor = HD ** (-0.5) * float(np.log2(np.e))
    lanes = lax.broadcasted_iota(jnp.int32, (N, HD), 1)
    st_parts[...] = jnp.zeros((3, 256, HD), F32)

    def send_stats(stage):
        for which, has in ((0, has_prev), (1, has_next)):
            st_send[stage, which] = jnp.transpose(st_parts[1 + which])[:16]
            pl.when(has)(lambda: stat_flow(stage, which).start())

    @pl.loop(0, HEADS)
    def _(h):
        ahead = AHEAD + h + h // 2
        pl.when(ahead < HEADS)(lambda: pass_on(ahead))
        ac_turn = ac_turned(h)
        flow(own_sib, h).wait_recv()
        flow(wd_sib, h).wait_recv()
        pl.when(inner)(lambda: flow(wd_ac, h).wait_recv())
        pl.when(jnp.logical_and(inner_from, jnp.logical_not(ac_turn)))(lambda: flow(ac_to, h).wait_recv())
        pl.when(jnp.logical_and(inner_from, ac_turn))(lambda: turn_flow(2, h).wait_recv())
        pl.when(has_from)(lambda: flow(wz_sib, h).wait_recv())
        pl.when(has_prev)(lambda: query_flow(0, h).wait_recv())
        pl.when(has_next)(lambda: query_flow(1, h).wait_recv())

        def attend(part, slots):
            keys = kv[:slots, h, :, :HD].reshape(slots * N, HD)
            values = jnp.concatenate(
                [kv[:slots, h, :, HD:].reshape(slots * N, HD), ones[:slots].reshape(slots * N, HD)], axis=1
            )
            scores = lax.dot_general(
                q[part, h], keys, (((1,), (1,)), ((), ())), preferred_element_type=F32
            )
            peak = jnp.max(scores, axis=-1, keepdims=True)
            expo = jnp.exp2((scores - peak) * factor).astype(BF16)
            acc = jnp.dot(expo, values, preferred_element_type=F32)
            stat = peak * factor + jnp.log2(acc[:, HD:])
            st_parts[part, :N] = jnp.where(lanes == h, stat, st_parts[part, :N])
            return acc[:, :HD] / acc[:, HD:]

        def other_frames(slots):
            for part in (1, 2):
                o_send[part - 1, h] = attend(part, slots).astype(BF16)

        def own_frames(slots):
            o_own[h] = attend(0, slots)

        pl.when(inner)(lambda: other_frames(SLOTS))
        pl.when(jnp.logical_not(inner))(lambda: other_frames(AC_WD))
        pl.when(has_prev)(lambda: result_flow(0, h).start())
        pl.when(has_next)(lambda: result_flow(1, h).start())
        pl.when(h + SHARE < HEADS)(lambda: share(h + SHARE))
        pl.when(jnp.logical_and(h % 2 == 1, ahead + 1 < HEADS))(lambda: pass_on(ahead + 1))
        pl.when(inner)(lambda: own_frames(SLOTS))
        pl.when(jnp.logical_not(inner))(lambda: own_frames(AC_WD))

        pl.when(h == EARLY - 1)(lambda: send_stats(0))

    send_stats(1)

    def collect(stage, first, last):
        for which, has in ((0, has_next), (1, has_prev)):

            @pl.when(has)
            def _():
                stat_flow(stage, which).wait_recv()

                @pl.loop(first, last)
                def _(h):
                    result_flow(which, h).wait_recv()

        below = jnp.zeros((HD - 16, 256), F32)
        l_prev = jnp.transpose(jnp.concatenate([st_recv[stage, 0], below], axis=0))[:N]
        l_next = jnp.transpose(jnp.concatenate([st_recv[stage, 1], below], axis=0))[:N]
        l_own = st_parts[0, :N]
        top = jnp.maximum(jnp.maximum(l_prev, l_next), l_own)
        e_prev, e_next, e_own = jnp.exp2(l_prev - top), jnp.exp2(l_next - top), jnp.exp2(l_own - top)
        total = 1.0 / (e_prev + e_next + e_own)
        e_prev, e_next, e_own = e_prev * total, e_next * total, e_own * total
        for h in range(first, last):
            column = slice(h, h + 1)
            att[:, h * HD : (h + 1) * HD] = (
                e_own[:, column] * o_own[h]
                + e_prev[:, column] * o_recv[0, h].astype(F32)
                + e_next[:, column] * o_recv[1, h].astype(F32)
            ).astype(BF16)

    split = EARLY * HD
    collect(0, 0, EARLY)
    for c in range(NCHUNK):
        weight_copy(3, c).wait()
        acc = jnp.dot(att[:, :split], wo[c, :split], preferred_element_type=F32)
        proj[2 * c] = acc[:, :HD]
        proj[2 * c + 1] = acc[:, HD:]

    collect(1, EARLY, HEADS)
    for c in range(NCHUNK):
        columns = slice(c * CHUNK, (c + 1) * CHUNK)
        early = jnp.concatenate([proj[2 * c], proj[2 * c + 1]], axis=1)
        out_ref[:, columns] = (
            (early + jnp.dot(att[:, split:], wo[c, split:], preferred_element_type=F32)) * mod_ref[2:3, columns]
        ).astype(BF16)

    @pl.loop(0, HEADS)
    def _(h):
        flow(own_wd, h).wait_send()
        flow(own_sib, h).wait_send()
        flow(wd_sib, h).wait_send()

        @pl.when(inner)
        def _():
            flow(own_ac, h).wait_send()
            flow(wd_ac, h).wait_send()

        turn, ac_turn = turned(h), ac_turned(h)
        pl.when(jnp.logical_and(has_to, jnp.logical_not(turn)))(lambda: flow(wd_to, h).wait_send())
        pl.when(jnp.logical_and(inner_to, jnp.logical_not(ac_turn)))(lambda: flow(ac_to, h).wait_send())
        pl.when(jnp.logical_and(has_from, in_transit(h)))(lambda: turn_flow(0, h).wait_send())
        pl.when(jnp.logical_and(has_to, turn))(lambda: turn_flow(1, h).wait_send())
        pl.when(jnp.logical_and(inner_to, ac_turn))(lambda: turn_flow(2, h).wait_send())
        pl.when(has_from)(lambda: flow(wz_sib, h).wait_send())

        @pl.when(has_next)
        def _():
            query_flow(0, h).wait_send()
            result_flow(1, h).wait_send()

        @pl.when(has_prev)
        def _():
            query_flow(1, h).wait_send()
            result_flow(0, h).wait_send()

    for stage in range(2):
        pl.when(has_prev)(lambda: stat_flow(stage, 0).wait_send())
        pl.when(has_next)(lambda: stat_flow(stage, 1).wait_send())


def body(tokens, modulation, w_query, w_key, w_value, w_out, norm_q, norm_k):
    vmem = pl.BlockSpec(memory_space=pltpu.VMEM)
    hbm = pl.BlockSpec(memory_space=pl.ANY)
    weight = pltpu.VMEM((NCHUNK, D, CHUNK), BF16)
    dma = pltpu.SemaphoreType.DMA
    result = pl.pallas_call(
        kernel,
        out_shape=jax.ShapeDtypeStruct((N, D), BF16),
        in_specs=[vmem] * 5 + [hbm] * 4,
        out_specs=vmem,
        scratch_shapes=[
            weight, weight, weight, weight,
            pltpu.VMEM((N, D), BF16),
            pltpu.VMEM((HEADS, N, HD), F32),
            pltpu.VMEM((N, 3 * HD), F32),
            pltpu.VMEM((SLOTS, HEADS, N, 2 * HD), BF16),
            pltpu.VMEM(((HEADS - AC_TURN) // 2, N, 2 * HD), BF16),
            pltpu.VMEM((SLOTS, N, HD), BF16),
            pltpu.VMEM((3, HEADS, N, HD), BF16),
            pltpu.VMEM((2, HEADS, N, HD), BF16),
            pltpu.VMEM((2, HEADS, N, HD), BF16),
            pltpu.VMEM((HEADS, N, HD), F32),
            pltpu.VMEM((2, 2, 16, 256), F32),
            pltpu.VMEM((2, 2, 16, 256), F32),
            pltpu.VMEM((3, 256, HD), F32),
            pltpu.VMEM((N, D), BF16),
            dma((4, NCHUNK)),
            dma((8, HEADS)), dma((8, HEADS)),
            dma((3, (HEADS - AC_TURN) // 2)), dma((3, (HEADS - AC_TURN) // 2)),
            dma((2, HEADS)), dma((2, HEADS)),
            dma((2, HEADS)), dma((2, HEADS)),
            dma((2, 2)), dma((2, 2)),
        ],
        compiler_params=pltpu.CompilerParams(
            collective_id=0, has_side_effects=True, vmem_limit_bytes=60 * 1024 * 1024
        ),
        name="tile_attention",
    )(
        tokens.reshape(N, D),
        modulation,
        norm_q,
        norm_k,
        jnp.asarray(angle_tables()),
        w_query, w_key, w_value, w_out,
    )
    return result.reshape(3, 8, 8, D)


def solution(mesh):
    in_specs = (P("ta", "ha", "wa", None), P(), P(), P(), P(), P(), P(), P())
    out_specs = P("ta", "ha", "wa", None)
    return jax.shard_map(body, mesh=mesh, in_specs=in_specs, out_specs=out_specs, check_vma=False)
```
